512 devices in a mesh: grp: 16 (over z), tp: 32 (over y, x, core).
Axes of the slice: x: 4, y: 4, z: 16, core: 2. Of those that a mesh axis runs over, the one named last changes fastest.
Arguments:
- inputs: bfloat16 [61440, 8192], P('grp', 'tp'), may hold values from -6 to 6
- cotangent: bfloat16 [61440, 8192], P('grp', 'tp'), may hold values from -0.059814453 to 0.059814453
- factor_a: bfloat16 [64, 8192, 128], P('grp', 'tp'), may hold values from -0.0625 to 0.0625
- factor_b: bfloat16 [64, 128, 8192], P('grp', None, 'tp'), may hold values from -0.5 to 0.5
- adapter_slot: int32 [64], replicated, may hold values from 0 to 63, as said below
- seg_adapter: int32 [16, 30], replicated, may hold values from 0 to 63, as said below
Outputs:
- factor_a_grad: bfloat16 [64, 8192, 128], P('grp', 'tp')
- factor_b_grad: bfloat16 [64, 128, 8192], P('grp', None, 'tp')
The draws below stay inside these ranges and needn't reach their ends.
Inputs may be any that keep to these rules, and one draw needn't show every extreme that they name: `adapter_slot`: A permutation: slot s lies on index s // 4 of grp. `seg_adapter`: within one micro-batch, all segments whose adapters' slots lie on the same index of grp use the same adapter.
All inputs are finite; a program needn't handle non-finite values.
Results may differ from the reference program's by a relative error of at most 0.0057.
Values may be sent and summed in bfloat16 or wider, within the bound.
A program may use at most 64 MiB of HBM per device.

```python
import jax
import jax.numpy as jnp
from jax import lax

D = 8192
R = 128
SEGLEN = 128
SEG = 30
OWN = 4
NA = 64
TOKENS = 61440
N_GRP = 16


def layout_draw(key):
    base = jax.random.fold_in(key, 31)
    keys = jax.random.split(base, 6)
    storage = jax.random.permutation(keys[0], NA)
    inverse = jnp.argsort(storage)
    local_pick = jax.random.randint(keys[1], (N_GRP, N_GRP), 0, OWN)
    order = jax.random.permutation(keys[2], N_GRP)
    first_draw = jax.random.randint(keys[3], (N_GRP, SEG), 0, N_GRP)
    second_draw = jax.random.randint(keys[4], (N_GRP, SEG), 0, N_GRP)
    owners = order[jnp.minimum(first_draw, second_draw)]
    spots = jax.random.randint(keys[5], (N_GRP, 1), 0, SEG)
    positions = jnp.arange(SEG)[None, :]
    owners = jnp.where(positions == spots, order[N_GRP - 1], owners)
    full_group = jax.random.randint(jax.random.fold_in(base, 5), (), 0, N_GRP)
    cover = order[positions % N_GRP]
    owners = jnp.where(jnp.arange(N_GRP)[:, None] == full_group, cover, owners)
    chosen = jnp.take_along_axis(local_pick, owners, axis=1)
    slots = owners * OWN + chosen
    adapters = inverse[slots]
    return (storage.astype(jnp.int32), adapters.astype(jnp.int32))


def draw_adapter_slot(key, part):
    return layout_draw(key)[0]


def draw_seg_adapter(key, part):
    return layout_draw(key)[1]


def block_levels(own_key, dims, pieces, least, high):
    gain, own = 1.0, jax.random.fold_in(own_key, 6)
    for axis_at, parts in pieces:
        draws = jnp.exp(jax.random.uniform(jax.random.fold_in(own, axis_at), (parts,), jnp.float32, least / len(pieces), high / len(pieces)))
        gain = gain * jnp.repeat(draws, dims[axis_at] // parts).reshape([-1 if axis == axis_at else 1 for axis in range(len(dims))])
    return gain


def bell_draw(own_key, dims, scale, limit, shards=(), dtype=jnp.bfloat16):
    array = scale * jax.random.normal(own_key, dims, jnp.float32)
    if shards:
        array = array * block_levels(own_key, dims, shards, -0.22, 0.18)
    return jnp.clip(array, -limit, limit).astype(dtype)


def setup_inputs(seed: int = 0) -> dict:
    key_list = jax.random.split(jax.random.key(seed), 7)
    inputs = bell_draw(key_list[0], (TOKENS, D), 1.0, 6.0, ((0, 16), (1, 32)))
    cotangent = bell_draw(key_list[1], (TOKENS, D), 0.01, 0.059814453, ((0, 16), (1, 32)))
    factor_a = bell_draw(key_list[2], (NA, D, R), D ** -0.5, 0.0625, ((0, 16), (1, 32)))
    factor_b = bell_draw(key_list[3], (NA, R, D), R ** -0.5, 0.5, ((0, 16), (2, 32)))
    adapter_slot = draw_adapter_slot(jax.random.fold_in(key_list[6], 71), 0)
    seg_adapter = draw_seg_adapter(jax.random.fold_in(key_list[6], 71), 0)
    return dict(inputs=inputs, cotangent=cotangent, factor_a=factor_a, factor_b=factor_b, adapter_slot=adapter_slot, seg_adapter=seg_adapter)


def reference(inputs, cotangent, factor_a, factor_b, adapter_slot, seg_adapter):
    slot_table = adapter_slot[seg_adapter].astype(jnp.int32)
    tok_blocks = inputs.reshape(N_GRP, SEG, SEGLEN, D)
    cot_blocks = cotangent.reshape(N_GRP, SEG, SEGLEN, D)

    def one_group(totals, item):
        tok_group, cot_group, slot_row = item
        seg_a = factor_a[slot_row].astype(jnp.float32)
        seg_b = factor_b[slot_row].astype(jnp.float32)
        tok_float = tok_group.astype(jnp.float32)
        cot_float = cot_group.astype(jnp.float32)
        low_input = jnp.einsum("std,sdr->str", tok_float, seg_a).astype(jnp.bfloat16)
        low_grad = jnp.einsum("std,srd->str", cot_float, seg_b).astype(jnp.bfloat16)
        grad_seg_a = jnp.einsum("std,str->sdr", tok_float, low_grad.astype(jnp.float32))
        grad_seg_b = jnp.einsum("str,std->srd", low_input.astype(jnp.float32), cot_float)
        part_a = jax.ops.segment_sum(grad_seg_a, slot_row, num_segments=NA)
        part_b = jax.ops.segment_sum(grad_seg_b, slot_row, num_segments=NA)
        part_a = lax.optimization_barrier(part_a.astype(jnp.bfloat16)).astype(jnp.float32)
        part_b = lax.optimization_barrier(part_b.astype(jnp.bfloat16)).astype(jnp.float32)
        return (totals[0] + part_a, totals[1] + part_b), None

    start = (jnp.zeros((NA, D, R), jnp.float32), jnp.zeros((NA, R, D), jnp.float32))
    totals, unused = lax.scan(one_group, start, (tok_blocks, cot_blocks, slot_table))
    return totals[0].astype(jnp.bfloat16), totals[1].astype(jnp.bfloat16)
```

```python
import functools

import jax
import jax.numpy as jnp
from jax import lax
from jax.experimental import pallas as pl
from jax.experimental.pallas import tpu as pltpu
from jax.sharding import PartitionSpec as P

MESH = pl.DeviceIdType.MESH
N = 16
OWN = 4
F32 = jnp.float32
BF16 = jnp.bfloat16
SEL, REL, PREV, LAST = 0, 256, 288, 320


def kernel(
    segs, chips, per,
    tab, x_hbm, c_hbm, fa, fb,
    oa, ob,
    xv, cv,
    gda, gdb, gsa, gsb, ssa, ssb, wa, wb,
    part, other, pair, pieces, low,
    ta, tb, ga, gb,
    rra, rrb, rda, rdb, sda, sdb,
    local_sem, gd_s, gd_r, gs_s, gs_r, rr_s, rr_r, rd_s, rd_r,
    c1_s, c1_r, rs_s, rs_r, ag_s, ag_r, c2_s, c2_r,
):
    me = lax.axis_index("grp")
    tp = lax.axis_index("tp")
    chip = tp // 2
    core = tp % 2
    half = chips * per
    mine = core * half
    theirs = (1 - core) * half
    up = {"grp": lax.rem(me + 1, N), "tp": tp}
    down = {"grp": lax.rem(me + N - 1, N), "tp": tp}
    nbr = (up, down)
    sib = {"grp": me, "tp": chip * 2 + 1 - core}

    def chip_dev(step):
        return {"grp": me, "tp": lax.rem(chip + step, chips) * 2 + core}

    def rcopy(src, dst, ss, rs, dev):
        return pltpu.make_async_remote_copy(
            src_ref=src, dst_ref=dst, send_sem=ss, recv_sem=rs,
            device_id=dev, device_id_type=MESH,
        )

    fac, gd, gs, ss, w, tok = (fb, fa), (gdb, gda), (gsb, gsa), (ssb, ssa), (wb, wa), (cv, xv)
    tot, grp, rr, rd, sd, out = (ta, tb), (ga, gb), (rra, rrb), (rda, rdb), (sda, sdb), (oa, ob)
    sign = (1, -1)

    def at(offset):
        return lax.rem(me + offset + 2 * N, N)

    def sel(g, o):
        return tab[SEL + g * N + o]

    barrier = pltpu.get_barrier_semaphore()
    for dev in (up, down, sib):
        pl.semaphore_signal(barrier, inc=1, device_id=dev, device_id_type=MESH)
    if chips > 1:
        @pl.loop(1, chips)
        def _(p):
            pl.semaphore_signal(barrier, inc=1, device_id=chip_dev(p), device_id_type=MESH)
    pl.semaphore_wait(barrier, 3 + chips - 1)

    def gd_copy(m, d, t, j, src):
        return rcopy(src, gd[m].at[d, t, j], gd_s.at[m, d, t, j], gd_r.at[m, d, t, j], nbr[d])

    def gather_first(m, j):
        for d in (0, 1):
            gd_copy(m, d, 0, j, fac[m].at[j]).start()

    def gather_dense(m, i):
        t, j = i // OWN, i % OWN
        for d in (0, 1):
            gd_copy(m, d, t, j, gd[m].at[d, t, j]).wait_recv()
            gd_copy(m, d, t + 1, j, gd[m].at[d, t, j]).start()

    def gs_copy(m, d, h, q, src):
        if q == 3:
            return rcopy(src.at[d], gs[m].at[d, h, q, d], gs_s.at[m, d, h, q], gs_r.at[m, d, h, q], nbr[d])
        return rcopy(src, gs[m].at[d, h, q], gs_s.at[m, d, h, q], gs_r.at[m, d, h, q], nbr[d])

    def pick(ref4, s):
        a = jnp.where(s == 0, ref4[0], ref4[1])
        b = jnp.where(s == 2, ref4[2], ref4[3])
        return jnp.where(s < 2, a, b)

    def gather_select(m):
        for d in (0, 1):
            for j in range(OWN):
                gd_copy(m, d, 3, j, gd[m].at[d, 3, j]).wait_recv()
            o = at(-4 * sign[d])
            for q in (3, 2, 1, 0):
                s = sel(at((q + 1) * sign[d]), o)
                ss[m][d, q] = pick(gd[m].at[d, 3], s)
                gs_copy(m, d, 0, q, ss[m].at[d, q]).start()

    def gather_tail(m, filler):
        for h in range(3):
            for q in range(3, h, -1):
                for d in (0, 1):
                    gs_copy(m, d, h, q, gs[m].at[d, h, q]).wait_recv()
                    gs_copy(m, d, h + 1, q, gs[m].at[d, h, q]).start()
            filler(h)
        for h in range(4):
            for d in (0, 1):
                gs_copy(m, d, h, h, gs[m].at[d, h, h]).wait_recv()

    def build(m):
        w[m][0] = pick(fac[m], sel(me, me))
        for d in (0, 1):
            for t in range(1, 5):
                w[m][(-t * sign[d]) % N] = pick(gd[m].at[d, t - 1], sel(me, at(-t * sign[d])))
            for h in range(3):
                w[m][(-(5 + h) * sign[d]) % N] = gs[m][d, h, h]
            w[m][8, d] = gs[m][d, 3, 3, d]

    def project(m, k):
        rows = tok[m][k]
        rel = tab[REL + k]
        if m == 0:
            f = w[m][rel].reshape(128, rows.shape[1])
            v = lax.dot_general(rows, f, (((1,), (1,)), ((), ())), preferred_element_type=F32)
        else:
            f = w[m][rel].reshape(rows.shape[1], 128)
            v = lax.dot_general(rows, f, (((1,), (0,)), ((), ())), preferred_element_type=F32)
        part[m, k] = v.astype(BF16)

    def core1(m):
        return rcopy(part.at[m, pl.ds(theirs, half)], other.at[m], c1_s.at[m], c1_r.at[m], sib)

    def rs_copy(m, p):
        dest = lax.rem(chip + p, chips)
        return rcopy(pair.at[m, pl.ds(dest * per, per)], pieces.at[m, p], rs_s.at[m, p], rs_r.at[m, p], chip_dev(p))

    def ag_copy(m, p):
        spot = low.at[m, pl.ds(mine + chip * per, per)]
        return rcopy(spot, spot, ag_s.at[m, p], ag_r.at[m, p], chip_dev(p))

    def ag_wait(m, p):
        src = lax.rem(chip - p + chips, chips)
        spot = low.at[m, pl.ds(mine + src * per, per)]
        rcopy(spot, spot, ag_s.at[m, p], ag_r.at[m, p], chip_dev(p)).wait_recv()

    def core2(m, base):
        spot = low.at[m, pl.ds(base, half)]
        return rcopy(spot, spot, c2_s.at[m], c2_r.at[m], sib)

    def reduce_start(m):
        core1(m).wait_recv()

        @pl.loop(0, half)
        def _(h):
            pair[m, h] = (part[m, mine + h].astype(F32) + other[m, h].astype(F32)).astype(BF16)

        if chips > 1:
            @pl.loop(1, chips)
            def _(p):
                rs_copy(m, p).start()

    def reduce_mid(m):
        if chips > 1:
            @pl.loop(1, chips)
            def _(p):
                rs_copy(m, p).wait_recv()
        for l in range(per):
            acc = pair[m, chip * per + l].astype(F32)
            if chips > 1:
                acc = lax.fori_loop(1, chips, lambda p, a: a + pieces[m, p, l].astype(F32), acc)
            low[m, mine + chip * per + l] = acc.astype(BF16)
        if chips > 1:
            @pl.loop(1, chips)
            def _(p):
                ag_copy(m, p).start()

    def reduce_end(m):
        if chips > 1:
            @pl.loop(1, chips)
            def _(p):
                ag_wait(m, p)
        core2(m, mine).start()

    def outer(r, k):
        prev = tab[PREV + k]
        if r == 0:
            v = lax.dot_general(xv[k], low[0, k], (((0,), (0,)), ((), ())), preferred_element_type=F32)
        else:
            v = lax.dot_general(low[1, k], cv[k], (((0,), (0,)), ((), ())), preferred_element_type=F32)
        tot[r][k] = tot[r][prev] + v

    def groups(r):
        @pl.loop(0, segs)
        def _(k):
            outer(r, k)

        @pl.loop(0, N)
        def _(g):
            grp[r][g] = tot[r][tab[LAST + g]].astype(BF16).reshape(grp[r].shape[1:])

    def rr_copy(r, d, h, q, src):
        if q == 3:
            return rcopy(src.at[d], rr[r].at[d, h, q, d], rr_s.at[r, d, h, q], rr_r.at[r, d, h, q], nbr[d])
        return rcopy(src, rr[r].at[d, h, q], rr_s.at[r, d, h, q], rr_r.at[r, d, h, q], nbr[d])

    def ret_own(r):
        for q in (3, 2, 1, 0):
            for d in (0, 1):
                rr_copy(r, d, 3 - q, q, grp[r].at[((5 + q) * sign[d]) % N]).start()

    def ret_raw(r):
        for h in range(3):
            for q in range(3, 2 - h, -1):
                for d in (0, 1):
                    rr_copy(r, d, h, q, rr[r].at[d, h, q]).wait_recv()
                    rr_copy(r, d, h + 1, q, rr[r].at[d, h, q]).start()

    def rd_copy(r, d, u, s):
        return rcopy(sd[r].at[d, u, s], rd[r].at[d, u, s], rd_s.at[r, d, u, s], rd_r.at[r, d, u, s], nbr[d])

    def masked(flag, v):
        return jnp.where(flag, v, jnp.zeros_like(v))

    def ret_combine(r):
        for d in (0, 1):
            for q in (3, 2, 1, 0):
                rr_copy(r, d, 3, q, rr[r].at[d, 3, q]).wait_recv()
            o = at(4 * sign[d])
            for s in range(OWN):
                acc = masked(sel(me, o) == s, grp[r][(4 * sign[d]) % N].astype(F32))
                for q in (0, 1, 2):
                    acc = acc + masked(sel(at(-(q + 1) * sign[d]), o) == s, rr[r][d, 3, q].astype(F32))
                far = masked(sel(at(-4 * sign[d]), o) == s, rr[r][d, 3, 3, d].astype(F32))
                sd[r][d, 0, s, d] = (acc[d] + far).astype(BF16)
                sd[r][d, 0, s, 1 - d] = acc[1 - d].astype(BF16)
                rd_copy(r, d, 0, s).start()

    def ret_dense(r, i):
        u, s = i // OWN, i % OWN
        for d in (0, 1):
            rd_copy(r, d, u, s).wait_recv()
            offset = (3 - u) * sign[d]
            own = grp[r][lax.rem(offset + N, N)].astype(F32)
            v = rd[r][d, u, s].astype(F32) + masked(sel(me, at(offset)) == s, own)
            sd[r][d, u + 1, s] = v.astype(BF16)
            rd_copy(r, d, u + 1, s).start()

    def ret_final(r):
        for s in range(OWN):
            v = masked(sel(me, me) == s, grp[r][0].astype(F32))
            for d in (0, 1):
                rd_copy(r, d, 3, s).wait_recv()
                v = v + rd[r][d, 3, s].astype(F32)
            out[r][s] = v.astype(BF16)

    def loop(lo, hi, f):
        if hi > lo:
            pl.loop(lo, hi)(f)

    for j in range(OWN):
        gather_first(0, j)
    copies = (
        pltpu.make_async_copy(c_hbm, cv, local_sem.at[0]),
        pltpu.make_async_copy(x_hbm, xv, local_sem.at[1]),
    )
    for cp in copies:
        cp.start()
    for r in (0, 1):
        tot[r][segs] = jnp.zeros(tot[r].shape[1:], F32)
        for k in range(segs, 2 * half):
            part[r, k] = jnp.zeros((128, 128), BF16)

    loop(0, 12, lambda i: gather_dense(0, i))
    gather_select(0)
    gather_first(1, 0)
    gather_tail(0, lambda h: gather_first(1, h + 1))
    build(0)
    for cp in copies:
        cp.wait()

    chunk = -(-segs // 3)

    def mixed(i):
        gather_dense(1, i)
        for e in range(chunk):
            k = i * chunk + e
            project(0, jnp.minimum(k, segs - 1) if chunk * 3 != segs else k)

    loop(0, 3, mixed)
    core1(0).start()
    loop(3, 5, lambda i: gather_dense(1, i))
    reduce_start(0)
    loop(5, 10, lambda i: gather_dense(1, i))
    reduce_mid(0)
    loop(10, 12, lambda i: gather_dense(1, i))
    gather_select(1)
    reduce_end(0)
    gather_tail(1, lambda h: None)
    build(1)
    core2(0, theirs).wait_recv()
    groups(0)
    ret_own(0)
    loop(0, segs, lambda k: project(1, k))
    core1(1).start()
    ret_raw(0)
    reduce_start(1)
    ret_combine(0)
    loop(0, 6, lambda i: ret_dense(0, i))
    reduce_mid(1)
    loop(6, 10, lambda i: ret_dense(0, i))
    reduce_end(1)
    loop(10, 12, lambda i: ret_dense(0, i))
    core2(1, theirs).wait_recv()
    groups(1)
    ret_own(1)
    ret_final(0)
    ret_raw(1)
    ret_combine(1)
    loop(0, 12, lambda i: ret_dense(1, i))
    ret_final(1)

    for m in (0, 1):
        core1(m).wait_send()
        core2(m, mine).wait_send()
        if chips > 1:
            @pl.loop(1, chips)
            def _(p):
                rs_copy(m, p).wait_send()
                ag_copy(m, p).wait_send()

        @pl.loop(0, 16)
        def _(i):
            for d in (0, 1):
                gd_copy(m, d, i // OWN, i % OWN, gd[m].at[d, 0, 0]).wait_send()
                rd_copy(m, d, i // OWN, i % OWN).wait_send()

        for d in (0, 1):
            for h in range(4):
                for q in range(3, h - 1, -1):
                    gs_copy(m, d, h, q, gs[m].at[d, h, q]).wait_send()
                for q in range(3, 2 - h, -1):
                    rr_copy(m, d, h, q, rr[m].at[d, h, q]).wait_send()


def tables(adapter_slot, seg_adapter):
    segs = seg_adapter.shape[1]
    me = lax.axis_index("grp")
    ids = jnp.arange(adapter_slot.shape[0], dtype=jnp.int32)
    hit = seg_adapter[:, :, None] == ids[None, None, :]
    slot = jnp.sum(jnp.where(hit, adapter_slot[None, None, :], 0), axis=2)
    owner, place = slot // OWN, slot % OWN
    groups = jnp.arange(N, dtype=jnp.int32)
    sel = jnp.max(jnp.where(owner[:, :, None] == groups[None, None, :], place[:, :, None], 0), axis=1)
    mine = lax.dynamic_slice_in_dim(owner, me, 1, 0)[0]
    rel = lax.rem(mine - me + N, N)
    ks = jnp.arange(segs, dtype=jnp.int32)
    before = (rel[:, None] == rel[None, :]) & (ks[None, :] < ks[:, None])
    prev = jnp.max(jnp.where(before, ks[None, :], -1), axis=1)
    prev = jnp.where(prev < 0, segs, prev)
    last = jnp.max(jnp.where(rel[None, :] == groups[:, None], ks[None, :], -1), axis=1)
    last = jnp.where(last < 0, segs, last)
    pad = jnp.zeros((32 - segs,), jnp.int32)
    return jnp.concatenate([sel.reshape(-1), rel, pad, prev, pad, last])


def body(chips, inputs, cotangent, factor_a, factor_b, adapter_slot, seg_adapter):
    segs = seg_adapter.shape[1]
    rows = inputs.shape[0] // segs
    feat = inputs.shape[1]
    per = -(-segs // (2 * chips))
    half = chips * per
    tab = tables(adapter_slot, seg_adapter)
    a_unit, b_unit = (2, feat // 2, 128), (2, 64, feat)
    bf = lambda *shape: pltpu.VMEM(shape, BF16)
    fl = lambda *shape: pltpu.VMEM(shape, F32)
    dma = lambda *shape: pltpu.SemaphoreType.DMA(shape)
    vm = pl.BlockSpec(memory_space=pltpu.VMEM)
    scratch = [
        bf(segs, rows, feat), bf(segs, rows, feat),
        bf(2, 4, 4, *a_unit), bf(2, 4, 4, *b_unit),
        bf(2, 4, 4, *a_unit), bf(2, 4, 4, *b_unit),
        bf(2, 4, *a_unit), bf(2, 4, *b_unit),
        bf(N, *a_unit), bf(N, *b_unit),
        bf(2, 2 * half, rows, 128), bf(2, half, rows, 128), bf(2, half, rows, 128),
        bf(2, chips, per, rows, 128), bf(2, 2 * half, rows, 128),
        fl(segs + 1, feat, 128), fl(segs + 1, 128, feat),
        bf(N, *a_unit), bf(N, *b_unit),
        bf(2, 4, 4, *a_unit), bf(2, 4, 4, *b_unit),
        bf(2, 4, 4, *a_unit), bf(2, 4, 4, *b_unit),
        bf(2, 4, 4, *a_unit), bf(2, 4, 4, *b_unit),
        dma(2),
    ] + [dma(2, 2, 4, 4)] * 8 + [
        dma(2), dma(2), dma(2, chips), dma(2, chips), dma(2, chips), dma(2, chips), dma(2), dma(2),
    ]
    grad_a, grad_b = pl.pallas_call(
        functools.partial(kernel, segs, chips, per),
        out_shape=(
            jax.ShapeDtypeStruct((OWN,) + a_unit, BF16),
            jax.ShapeDtypeStruct((OWN,) + b_unit, BF16),
        ),
        in_specs=[
            pl.BlockSpec(memory_space=pltpu.SMEM),
            pl.BlockSpec(memory_space=pl.ANY),
            pl.BlockSpec(memory_space=pl.ANY),
            vm, vm,
        ],
        out_specs=(vm, vm),
        scratch_shapes=scratch,
        compiler_params=pltpu.CompilerParams(
            collective_id=0, has_side_effects=True, vmem_limit_bytes=60 << 20
        ),
        name="adapter_backward",
    )(
        tab,
        inputs.reshape(segs, rows, feat),
        cotangent.reshape(segs, rows, feat),
        factor_a.reshape((OWN,) + a_unit),
        factor_b.reshape((OWN,) + b_unit),
    )
    return grad_a.reshape(factor_a.shape), grad_b.reshape(factor_b.shape)


def solution(mesh):
    return jax.shard_map(
        functools.partial(body, mesh.shape["tp"] // 2),
        mesh=mesh,
        in_specs=(
            P("grp", "tp"),
            P("grp", "tp"),
            P("grp", "tp", None),
            P("grp", None, "tp"),
            P(),
            P(),
        ),
        out_specs=(P("grp", "tp", None), P("grp", None, "tp")),
        check_vma=False,
    )
```

```python
import functools

import jax
import jax.numpy as jnp
from jax import lax
from jax.experimental import pallas as pl
from jax.experimental.pallas import tpu as pltpu
from jax.sharding import PartitionSpec as P

MESH = pl.DeviceIdType.MESH
N = 16
OWN = 4
F32 = jnp.float32
BF16 = jnp.bfloat16
REL, LAST = 16, 48


def kernel(
    segs, chips, per,
    aslot, seg, x_hbm, c_hbm, fa, fb,
    oa, ob,
    xv, cv,
    gda, gdb, gsa, gsb, ssa, ssb, wa, wb,
    part, other, pair, pieces, low,
    ta, tb, ga, gb,
    rra, rrb, rda, rdb, sda, sdb,
    vtab, tab,
    local_sem, gd_s, gd_r, gs_s, gs_r, rr_s, rr_r, rd_s, rd_r,
    c1_s, c1_r, rs_s, rs_r, ag_s, ag_r, c2_s, c2_r,
):
    me = lax.axis_index("grp")
    tp = lax.axis_index("tp")
    chip = tp // 2
    core = tp % 2
    half = chips * per
    mine = core * half
    theirs = (1 - core) * half
    up = {"grp": lax.rem(me + 1, N), "tp": tp}
    down = {"grp": lax.rem(me + N - 1, N), "tp": tp}
    nbr = (up, down)
    sib = {"grp": me, "tp": chip * 2 + 1 - core}

    def chip_dev(step):
        return {"grp": me, "tp": lax.rem(chip + step, chips) * 2 + core}

    def rcopy(src, dst, ss, rs, dev):
        return pltpu.make_async_remote_copy(
            src_ref=src, dst_ref=dst, send_sem=ss, recv_sem=rs,
            device_id=dev, device_id_type=MESH,
        )

    fac, gd, gs, ss, w, tok = (fb, fa), (gdb, gda), (gsb, gsa), (ssb, ssa), (wb, wa), (cv, xv)
    tot, grp, rr, rd, sd, out = (ta, tb), (ga, gb), (rra, rrb), (rda, rdb), (sda, sdb), (oa, ob)
    sign = (1, -1)

    def at(offset):
        return lax.rem(me + offset + 2 * N, N)

    def sel(g, o):
        return tab[g, o]

    barrier = pltpu.get_barrier_semaphore()
    for dev in (up, down, sib):
        pl.semaphore_signal(barrier, inc=1, device_id=dev, device_id_type=MESH)
    if chips > 1:
        @pl.loop(1, chips)
        def _(p):
            pl.semaphore_signal(barrier, inc=1, device_id=chip_dev(p), device_id_type=MESH)
    pl.semaphore_wait(barrier, 3 + chips - 1)

    def build_tables():
        ids = seg[...]
        zero = jnp.zeros_like(ids)
        slot = lax.fori_loop(0, aslot.shape[0], lambda n, a: jnp.where(ids == n, aslot[n], a), zero)
        owner, place = lax.shift_right_logical(slot, 2), slot & 3

        def iota(rows, cols, dim):
            return lax.broadcasted_iota(jnp.int32, (rows, cols), dim)

        lane = iota(N, 128, 1)
        chosen = jnp.zeros((N, 128), jnp.int32)
        for o in range(N):
            best = jnp.max(jnp.where(owner == o, place, 0), axis=1, keepdims=True)
            chosen = jnp.where(lane == o, best, chosen)
        vtab[0:N] = chosen
        row = jnp.sum(jnp.where(iota(N, segs, 0) == me, owner, 0), axis=0, keepdims=True)
        row = (row - me + N) & (N - 1)
        wide = jnp.broadcast_to(row, (32, segs))
        down32, right32 = iota(32, segs, 0), iota(32, segs, 1)
        col = jnp.sum(jnp.where(down32 == right32, wide, 0), axis=1, keepdims=True)
        prev = jnp.max(jnp.where((wide == col) & (right32 < down32), right32, -1), axis=1, keepdims=True)
        prev = jnp.where(prev < 0, segs, prev)
        vtab[REL:REL + 32] = jnp.where(iota(32, 128, 1) == 0, col, prev)
        last = jnp.max(jnp.where(wide[0:N] == iota(N, segs, 0), iota(N, segs, 1), -1), axis=1, keepdims=True)
        last = jnp.where(last < 0, segs, last)
        vtab[LAST:LAST + N] = jnp.broadcast_to(last, (N, 128))
        move = pltpu.make_async_copy(vtab, tab, local_sem.at[2])
        move.start()
        return move

    def spot(h, q):
        return (0, 4, 7, 9)[h] + q - h

    def gd_copy(m, d, t, j, src):
        return rcopy(src, gd[m].at[d, t, j], gd_s.at[m, d], gd_r.at[m, d, t, j], nbr[d])

    def gather_first(m, j):
        for d in (0, 1):
            gd_copy(m, d, 0, j, fac[m].at[j]).start()

    def gather_dense(m, i):
        t, j = i // OWN, i % OWN
        for d in (0, 1):
            gd_copy(m, d, t, j, gd[m].at[d, t, j]).wait_recv()
            gd_copy(m, d, t + 1, j, gd[m].at[d, t, j]).start()

    def gs_copy(m, d, h, q, src):
        if q == 3:
            return rcopy(src.at[d], gs[m].at[d, h, q, d], gs_s.at[m, d], gs_r.at[m, d, spot(h, q)], nbr[d])
        return rcopy(src, gs[m].at[d, h, q], gs_s.at[m, d], gs_r.at[m, d, spot(h, q)], nbr[d])

    def pick(ref4, s):
        a = jnp.where(s == 0, ref4[0], ref4[1])
        b = jnp.where(s == 2, ref4[2], ref4[3])
        return jnp.where(s < 2, a, b)

    def gather_select(m):
        for d in (0, 1):
            for j in range(OWN):
                gd_copy(m, d, 3, j, gd[m].at[d, 3, j]).wait_recv()
            o = at(-4 * sign[d])
            for q in (3, 2, 1, 0):
                s = sel(at((q + 1) * sign[d]), o)
                ss[m][d, q] = pick(gd[m].at[d, 3], s)
                gs_copy(m, d, 0, q, ss[m].at[d, q]).start()

    def gather_tail(m, filler):
        for h in range(3):
            for q in range(3, h, -1):
                for d in (0, 1):
                    gs_copy(m, d, h, q, gs[m].at[d, h, q]).wait_recv()
                    gs_copy(m, d, h + 1, q, gs[m].at[d, h, q]).start()
            filler(h)
        for h in range(4):
            for d in (0, 1):
                gs_copy(m, d, h, h, gs[m].at[d, h, h]).wait_recv()

    def build(m):
        w[m][0] = pick(fac[m], sel(me, me))
        for d in (0, 1):
            for t in range(1, 5):
                w[m][(-t * sign[d]) % N] = pick(gd[m].at[d, t - 1], sel(me, at(-t * sign[d])))
            for h in range(3):
                w[m][(-(5 + h) * sign[d]) % N] = gs[m][d, h, h]
            w[m][8, d] = gs[m][d, 3, 3, d]

    def project(m, k):
        rows = tok[m][k]
        rel = tab[REL + k, 0]
        if m == 0:
            f = w[m][rel].reshape(128, rows.shape[1])
            v = lax.dot_general(rows, f, (((1,), (1,)), ((), ())), preferred_element_type=F32)
        else:
            f = w[m][rel].reshape(rows.shape[1], 128)
            v = lax.dot_general(rows, f, (((1,), (0,)), ((), ())), preferred_element_type=F32)
        part[m, k] = v

    def core1(m):
        return rcopy(part.at[m, pl.ds(theirs, half)], other.at[m], c1_s.at[m], c1_r.at[m], sib)

    def rs_copy(m, p):
        dest = lax.rem(chip + p, chips)
        return rcopy(pair.at[m, pl.ds(dest * per, per)], pieces.at[m, p], rs_s.at[m], rs_r.at[m], chip_dev(p))

    def ag_copy(m, p):
        spot = low.at[m, pl.ds(mine + chip * per, per)]
        return rcopy(spot, spot, ag_s.at[m], ag_r.at[m], chip_dev(p))

    def core2(m, base):
        spot = low.at[m, pl.ds(base, half)]
        return rcopy(spot, spot, c2_s.at[m], c2_r.at[m], sib)

    def reduce_start(m):
        core1(m).wait_recv()

        @pl.loop(0, half)
        def _(h):
            pair[m, h] = (part[m, mine + h] + other[m, h]).astype(BF16)

        if chips > 1:
            @pl.loop(1, chips)
            def _(p):
                rs_copy(m, p).start()

    def pieces_of(m, ss, rs):
        span = pieces.at[m, pl.ds(1, chips - 1)]
        return rcopy(span, span, ss.at[m], rs.at[m], sib)

    def reduce_mid(m):
        if chips > 1:
            pieces_of(m, rs_s, rs_r).wait_recv()
        for l in range(per):
            acc = pair[m, chip * per + l].astype(F32)
            if chips > 1:
                acc = lax.fori_loop(1, chips, lambda p, a: a + pieces[m, p, l].astype(F32), acc)
            low[m, mine + chip * per + l] = acc.astype(BF16)
        if chips > 1:
            @pl.loop(1, chips)
            def _(p):
                ag_copy(m, p).start()

    def reduce_end(m):
        if chips > 1:
            pieces_of(m, ag_s, ag_r).wait_recv()
        core2(m, mine).start()

    def outer(r, k):
        if r == 0:
            return lax.dot_general(xv[k], low[0, k], (((0,), (0,)), ((), ())), preferred_element_type=F32)
        return lax.dot_general(low[1, k], cv[k], (((0,), (0,)), ((), ())), preferred_element_type=F32)

    third = segs // 3
    step = 5 if third % 5 == 0 else 1

    def outer_third(r, part_no):
        @pl.loop(0, third // step)
        def _(i):
            ks = [part_no * third + i * step + e for e in range(step)]
            vs = [outer(r, k) for k in ks]
            for k, v in zip(ks, vs):
                tot[r][k] = tot[r][tab[REL + k, 1]] + v

    def project_third(m, part_no):
        for e in range(third):
            project(m, part_no * third + e)

    def groups(r):
        @pl.loop(0, N // 4)
        def _(i):
            for e in range(4):
                g = i * 4 + e
                grp[r][g] = tot[r][tab[LAST + g, 0]].astype(BF16).reshape(grp[r].shape[1:])

    def rr_copy(r, d, h, q, src):
        if q == 3:
            return rcopy(src.at[d], rr[r].at[d, h, q, d], rr_s.at[r, d], rr_r.at[r, d, spot(3 - h, q)], nbr[d])
        return rcopy(src, rr[r].at[d, h, q], rr_s.at[r, d], rr_r.at[r, d, spot(3 - h, q)], nbr[d])

    def ret_own(r):
        for q in (3, 2, 1, 0):
            for d in (0, 1):
                rr_copy(r, d, 3 - q, q, grp[r].at[((5 + q) * sign[d]) % N]).start()

    def ret_raw(r, h):
        for q in range(3, 2 - h, -1):
            for d in (0, 1):
                rr_copy(r, d, h, q, rr[r].at[d, h, q]).wait_recv()
                rr_copy(r, d, h + 1, q, rr[r].at[d, h, q]).start()

    def rd_copy(r, d, u, s):
        return rcopy(sd[r].at[d, u, s], rd[r].at[d, u, s], rd_s.at[r, d], rd_r.at[r, d, u, s], nbr[d])

    def masked(flag, v):
        return jnp.where(flag, v, jnp.zeros_like(v))

    def ret_combine(r):
        for d in (0, 1):
            for q in (3, 2, 1, 0):
                rr_copy(r, d, 3, q, rr[r].at[d, 3, q]).wait_recv()
            o = at(4 * sign[d])
            for s in range(OWN):
                acc = masked(sel(me, o) == s, grp[r][(4 * sign[d]) % N].astype(F32))
                for q in (0, 1, 2):
                    acc = acc + masked(sel(at(-(q + 1) * sign[d]), o) == s, rr[r][d, 3, q].astype(F32))
                far = masked(sel(at(-4 * sign[d]), o) == s, rr[r][d, 3, 3, d].astype(F32))
                sd[r][d, 0, s, d] = (acc[d] + far).astype(BF16)
                sd[r][d, 0, s, 1 - d] = acc[1 - d].astype(BF16)
                rd_copy(r, d, 0, s).start()

    def ret_dense(r, i):
        u, s = i // OWN, i % OWN
        for d in (0, 1):
            rd_copy(r, d, u, s).wait_recv()
            offset = (3 - u) * sign[d]
            own = grp[r][lax.rem(offset + N, N)].astype(F32)
            v = rd[r][d, u, s].astype(F32) + masked(sel(me, at(offset)) == s, own)
            sd[r][d, u + 1, s] = v.astype(BF16)
            rd_copy(r, d, u + 1, s).start()

    def ret_final(r):
        for s in range(OWN):
            v = masked(sel(me, me) == s, grp[r][0].astype(F32))
            for d in (0, 1):
                rd_copy(r, d, 3, s).wait_recv()
                v = v + rd[r][d, 3, s].astype(F32)
            out[r][s] = v.astype(BF16)

    def loop(lo, hi, f):
        if hi > lo:
            pl.loop(lo, hi)(f)

    copies = (
        pltpu.make_async_copy(c_hbm, cv, local_sem.at[0]),
        pltpu.make_async_copy(x_hbm, xv, local_sem.at[1]),
    )
    for j in range(OWN):
        gather_first(0, j)
    for cp in copies:
        cp.start()
    move = build_tables()
    loop(0, 4, lambda i: gather_dense(0, i))
    for r in (0, 1):
        tot[r][segs] = jnp.zeros(tot[r].shape[1:], F32)
        for k in range(segs, 2 * half):
            part[r, k] = jnp.zeros((128, 128), F32)
    move.wait()
    for cp in copies:
        cp.wait()
    loop(4, 12, lambda i: gather_dense(0, i))
    gather_select(0)
    gather_first(1, 0)
    gather_tail(0, lambda h: gather_first(1, h + 1))
    build(0)

    def mixed(i):
        gather_dense(1, i)
        project_third(0, i)

    loop(0, 3, mixed)
    core1(0).start()
    loop(3, 5, lambda i: gather_dense(1, i))
    reduce_start(0)
    loop(5, 10, lambda i: gather_dense(1, i))
    reduce_mid(0)
    loop(10, 12, lambda i: gather_dense(1, i))
    gather_select(1)
    reduce_end(0)

    def fill(h):
        if h == 0:
            core2(0, theirs).wait_recv()
        outer_third(0, h)

    gather_tail(1, fill)
    groups(0)
    ret_own(0)
    build(1)
    project_third(1, 0)
    ret_raw(0, 0)
    project_third(1, 1)
    ret_raw(0, 1)
    project_third(1, 2)
    core1(1).start()
    ret_raw(0, 2)
    ret_combine(0)
    loop(0, 1, lambda i: ret_dense(0, i))
    reduce_start(1)
    loop(1, 6, lambda i: ret_dense(0, i))
    reduce_mid(1)
    loop(6, 10, lambda i: ret_dense(0, i))
    reduce_end(1)
    loop(10, 11, lambda i: ret_dense(0, i))
    core2(1, theirs).wait_recv()
    outer_third(1, 0)
    loop(11, 12, lambda i: ret_dense(0, i))
    outer_third(1, 1)
    outer_third(1, 2)
    groups(1)
    ret_own(1)
    ret_final(0)
    for h in range(3):
        ret_raw(1, h)
    ret_combine(1)
    loop(0, 12, lambda i: ret_dense(1, i))
    ret_final(1)

    for m in (0, 1):
        core1(m).wait_send()
        core2(m, mine).wait_send()
        if chips > 1:
            pieces_of(m, rs_s, rs_r).wait_send()
            pieces_of(m, ag_s, ag_r).wait_send()
        for d in (0, 1):
            for buf, sem in ((gd, gd_s), (rd, rd_s)):
                rcopy(buf[m].at[d], buf[m].at[d], sem.at[m, d], sem.at[m, d], nbr[d]).wait_send()
            for buf, sem in ((gs, gs_s), (rr, rr_s)):
                span = buf[m].at[d, pl.ds(0, 2)]
                rcopy(span, span, sem.at[m, d], sem.at[m, d], nbr[d]).wait_send()


def body(chips, inputs, cotangent, factor_a, factor_b, adapter_slot, seg_adapter):
    segs = seg_adapter.shape[1]
    rows = inputs.shape[0] // segs
    feat = inputs.shape[1]
    per = -(-segs // (2 * chips))
    half = chips * per
    a_unit, b_unit = (2, feat // 2, 128), (2, 64, feat)
    bf = lambda *shape: pltpu.VMEM(shape, BF16)
    fl = lambda *shape: pltpu.VMEM(shape, F32)
    dma = lambda *shape: pltpu.SemaphoreType.DMA(shape)
    vm = pl.BlockSpec(memory_space=pltpu.VMEM)
    scratch = [
        bf(segs, rows, feat), bf(segs, rows, feat),
        bf(2, 4, 4, *a_unit), bf(2, 4, 4, *b_unit),
        bf(2, 4, 4, *a_unit), bf(2, 4, 4, *b_unit),
        bf(2, 4, *a_unit), bf(2, 4, *b_unit),
        bf(N, *a_unit), bf(N, *b_unit),
        fl(2, 2 * half, rows, 128), fl(2, half, rows, 128), bf(2, half, rows, 128),
        bf(2, chips, per, rows, 128), bf(2, 2 * half, rows, 128),
        fl(segs + 1, feat, 128), fl(segs + 1, 128, feat),
        bf(N, *a_unit), bf(N, *b_unit),
        bf(2, 4, 4, *a_unit), bf(2, 4, 4, *b_unit),
        bf(2, 4, 4, *a_unit), bf(2, 4, 4, *b_unit),
        bf(2, 4, 4, *a_unit), bf(2, 4, 4, *b_unit),
        pltpu.VMEM((64, 128), jnp.int32), pltpu.SMEM((64, 128), jnp.int32),
        dma(3),
        dma(2, 2), dma(2, 2, 4, 4), dma(2, 2), dma(2, 2, 10),
        dma(2, 2), dma(2, 2, 10), dma(2, 2), dma(2, 2, 4, 4),
    ] + [dma(2)] * 8
    grad_a, grad_b = pl.pallas_call(
        functools.partial(kernel, segs, chips, per),
        out_shape=(
            jax.ShapeDtypeStruct((OWN,) + a_unit, BF16),
            jax.ShapeDtypeStruct((OWN,) + b_unit, BF16),
        ),
        in_specs=[
            pl.BlockSpec(memory_space=pltpu.SMEM),
            vm,
            pl.BlockSpec(memory_space=pl.ANY),
            pl.BlockSpec(memory_space=pl.ANY),
            vm, vm,
        ],
        out_specs=(vm, vm),
        scratch_shapes=scratch,
        compiler_params=pltpu.CompilerParams(
            collective_id=0, has_side_effects=True, vmem_limit_bytes=60 << 20
        ),
        name="adapter_backward",
    )(
        adapter_slot,
        seg_adapter,
        inputs.reshape(segs, rows, feat),
        cotangent.reshape(segs, rows, feat),
        factor_a.reshape((OWN,) + a_unit),
        factor_b.reshape((OWN,) + b_unit),
    )
    return grad_a.reshape(factor_a.shape), grad_b.reshape(factor_b.shape)


def solution(mesh):
    return jax.shard_map(
        functools.partial(body, mesh.shape["tp"] // 2),
        mesh=mesh,
        in_specs=(
            P("grp", "tp"),
            P("grp", "tp"),
            P("grp", "tp", None),
            P("grp", None, "tp"),
            P(),
            P(),
        ),
        out_specs=(P("grp", "tp", None), P("grp", None, "tp")),
        check_vma=False,
    )
```

```python
import functools
import math

import jax
import jax.numpy as jnp
from jax import lax
from jax.experimental import pallas as pl
from jax.experimental.pallas import tpu as pltpu
from jax.sharding import PartitionSpec as P

MESH = pl.DeviceIdType.MESH
N = 16
OWN = 4
F32 = jnp.float32
BF16 = jnp.bfloat16
REL, LAST = 16, 48


def kernel(
    segs, chips, per,
    aslot, seg, x_hbm, c_hbm, fa, fb,
    oa, ob,
    xv, cv,
    gda, gdb, gsa, gsb, ssa, ssb, wa, wb,
    part, other, pair, pieces, low,
    ta, tb, ga, gb,
    rra, rrb, rda, rdb, sda, sdb,
    vtab, tab,
    local_sem, gd_s, gd_r, gs_s, gs_r, rr_s, rr_r, rd_s, rd_r,
    c1_s, c1_r, rs_s, rs_r, ag_s, ag_r, c2_s, c2_r,
):
    me = lax.axis_index("grp")
    tp = lax.axis_index("tp")
    chip = tp // 2
    core = tp % 2
    half = chips * per
    mine = core * half
    theirs = (1 - core) * half
    up = {"grp": lax.rem(me + 1, N), "tp": tp}
    down = {"grp": lax.rem(me + N - 1, N), "tp": tp}
    nbr = (up, down)
    sib = {"grp": me, "tp": chip * 2 + 1 - core}

    side = math.isqrt(chips)

    def hops(step):
        return sum(min(e, side - e) for e in divmod(step, side))

    others = sorted(range(1, chips), key=lambda step: -hops(step))

    def chip_at(step):
        dy, dx = divmod(step, side)
        return lax.rem(chip // side + dy, side) * side + lax.rem(chip % side + dx, side)

    def chip_dev(step):
        return {"grp": me, "tp": chip_at(step) * 2 + core}

    def rcopy(src, dst, ss, rs, dev):
        return pltpu.make_async_remote_copy(
            src_ref=src, dst_ref=dst, send_sem=ss, recv_sem=rs,
            device_id=dev, device_id_type=MESH,
        )

    fac, gd, gs, ss, w, tok = (fb, fa), (gdb, gda), (gsb, gsa), (ssb, ssa), (wb, wa), (cv, xv)
    tot, grp, rr, rd, sd, out = (ta, tb), (ga, gb), (rra, rrb), (rda, rdb), (sda, sdb), (oa, ob)
    sign = (1, -1)

    def at(offset):
        return lax.rem(me + offset + 2 * N, N)

    def sel(g, o):
        return tab[g, o]

    barrier = pltpu.get_barrier_semaphore()
    for dev in (up, down, sib):
        pl.semaphore_signal(barrier, inc=1, device_id=dev, device_id_type=MESH)
    for p in others:
        pl.semaphore_signal(barrier, inc=1, device_id=chip_dev(p), device_id_type=MESH)
    pl.semaphore_wait(barrier, 3 + chips - 1)

    def build_tables():
        ids = seg[...]
        zero = jnp.zeros_like(ids)
        slot = lax.fori_loop(0, aslot.shape[0], lambda n, a: jnp.where(ids == n, aslot[n], a), zero)
        owner, place = lax.shift_right_logical(slot, 2), slot & 3

        def iota(rows, cols, dim):
            return lax.broadcasted_iota(jnp.int32, (rows, cols), dim)

        lane = iota(N, 128, 1)
        chosen = jnp.zeros((N, 128), jnp.int32)
        for o in range(N):
            best = jnp.max(jnp.where(owner == o, place, 0), axis=1, keepdims=True)
            chosen = jnp.where(lane == o, best, chosen)
        vtab[0:N] = chosen
        row = jnp.sum(jnp.where(iota(N, segs, 0) == me, owner, 0), axis=0, keepdims=True)
        row = (row - me + N) & (N - 1)
        wide = jnp.broadcast_to(row, (32, segs))
        down32, right32 = iota(32, segs, 0), iota(32, segs, 1)
        col = jnp.sum(jnp.where(down32 == right32, wide, 0), axis=1, keepdims=True)
        size = 2 * half

        def turn(k):
            return jnp.where(k >= mine, k - mine, k - mine + size)

        def back(best):
            k = best + mine
            return jnp.where(best < 0, size, jnp.where(k >= size, k - size, k))

        right_turn, down_turn = turn(right32), turn(down32)
        prev = back(jnp.max(
            jnp.where((wide == col) & (right_turn < down_turn), right_turn, -1), axis=1, keepdims=True
        ))
        vtab[REL:REL + 32] = jnp.where(iota(32, 128, 1) == 0, col, prev)
        last = back(jnp.max(
            jnp.where(wide[0:N] == iota(N, segs, 0), right_turn[0:N], -1), axis=1, keepdims=True
        ))
        vtab[LAST:LAST + N] = jnp.broadcast_to(last, (N, 128))
        move = pltpu.make_async_copy(vtab, tab, local_sem.at[2])
        move.start()
        return move

    def spot(h, q):
        return (0, 4, 7, 9)[h] + q - h

    def gd_copy(m, d, t, j, src):
        return rcopy(src, gd[m].at[d, t, j], gd_s.at[m, d], gd_r.at[m, d, t, j], nbr[d])

    def gather_first(m, j):
        for d in (0, 1):
            gd_copy(m, d, 0, j, fac[m].at[j]).start()

    def gather_dense(m, i):
        t, j = i // OWN, i % OWN
        for d in (0, 1):
            gd_copy(m, d, t, j, gd[m].at[d, t, j]).wait_recv()
            gd_copy(m, d, t + 1, j, gd[m].at[d, t, j]).start()

    def gs_copy(m, d, h, q, src):
        if q == 3:
            return rcopy(src.at[d], gs[m].at[d, h, q, d], gs_s.at[m, d], gs_r.at[m, d, spot(h, q)], nbr[d])
        return rcopy(src, gs[m].at[d, h, q], gs_s.at[m, d], gs_r.at[m, d, spot(h, q)], nbr[d])

    def pick(ref4, s):
        a = jnp.where(s == 0, ref4[0], ref4[1])
        b = jnp.where(s == 2, ref4[2], ref4[3])
        return jnp.where(s < 2, a, b)

    def gather_select(m):
        for d in (0, 1):
            for j in range(OWN):
                gd_copy(m, d, 3, j, gd[m].at[d, 3, j]).wait_recv()
            o = at(-4 * sign[d])
            for q in (3, 2, 1, 0):
                s = sel(at((q + 1) * sign[d]), o)
                ss[m][d, q] = pick(gd[m].at[d, 3], s)
                gs_copy(m, d, 0, q, ss[m].at[d, q]).start()

    def gather_tail(m, filler):
        for h in range(3):
            for q in range(3, h, -1):
                for d in (0, 1):
                    gs_copy(m, d, h, q, gs[m].at[d, h, q]).wait_recv()
                    gs_copy(m, d, h + 1, q, gs[m].at[d, h, q]).start()
            filler(h)
        for h in range(4):
            for d in (0, 1):
                gs_copy(m, d, h, h, gs[m].at[d, h, h]).wait_recv()

    def build(m):
        w[m][0] = pick(fac[m], sel(me, me))
        for d in (0, 1):
            for t in range(1, 5):
                w[m][(-t * sign[d]) % N] = pick(gd[m].at[d, t - 1], sel(me, at(-t * sign[d])))
            for h in range(3):
                w[m][(-(5 + h) * sign[d]) % N] = gs[m][d, h, h]
            w[m][8, d] = gs[m][d, 3, 3, d]

    def project(m, k):
        rows = tok[m][jnp.minimum(k, segs - 1)]
        rel = tab[REL + k, 0]
        if m == 0:
            f = w[m][rel].reshape(128, rows.shape[1])
            v = lax.dot_general(rows, f, (((1,), (1,)), ((), ())), preferred_element_type=F32)
        else:
            f = w[m][rel].reshape(rows.shape[1], 128)
            v = lax.dot_general(rows, f, (((1,), (0,)), ((), ())), preferred_element_type=F32)
        part[m, k] = v

    def core1(m):
        return rcopy(part.at[m, pl.ds(theirs, half)], other.at[m], c1_s.at[m], c1_r.at[m], sib)

    def rs_copy(m, p):
        dest = chip_at(p)
        return rcopy(pair.at[m, pl.ds(dest * per, per)], pieces.at[m, p], rs_s.at[m], rs_r.at[m], chip_dev(p))

    def ag_copy(m, p):
        spot = low.at[m, pl.ds(mine + chip * per, per)]
        return rcopy(spot, spot, ag_s.at[m], ag_r.at[m], chip_dev(p))

    def core2(m, base):
        spot = low.at[m, pl.ds(base, half)]
        return rcopy(spot, spot, c2_s.at[m], c2_r.at[m], sib)

    def reduce_start(m):
        core1(m).wait_recv()

        @pl.loop(0, half)
        def _(h):
            pair[m, h] = (part[m, mine + h] + other[m, h]).astype(BF16)

        for p in others:
            rs_copy(m, p).start()

    def pieces_of(m, ss, rs):
        span = pieces.at[m, pl.ds(1, chips - 1)]
        return rcopy(span, span, ss.at[m], rs.at[m], sib)

    def reduce_mid(m):
        if chips > 1:
            pieces_of(m, rs_s, rs_r).wait_recv()
        for l in range(per):
            acc = pair[m, chip * per + l].astype(F32)
            if chips > 1:
                acc = lax.fori_loop(1, chips, lambda p, a: a + pieces[m, p, l].astype(F32), acc)
            low[m, mine + chip * per + l] = acc.astype(BF16)
        for p in others:
            ag_copy(m, p).start()

    def reduce_end(m):
        if chips > 1:
            pieces_of(m, ag_s, ag_r).wait_recv()
        core2(m, mine).start()

    def outer(r, k):
        if r == 0:
            return lax.dot_general(xv[jnp.minimum(k, segs - 1)], low[0, k], (((0,), (0,)), ((), ())), preferred_element_type=F32)
        return lax.dot_general(low[1, k], cv[jnp.minimum(k, segs - 1)], (((0,), (0,)), ((), ())), preferred_element_type=F32)

    quarter = -(-half // 2)
    step = 4 if half % 8 == 0 else 1

    def spans(base, part_no):
        return base + part_no * quarter, min(quarter, half - part_no * quarter)

    def outer_part(r, base, part_no):
        lo, count = spans(base, part_no)

        @pl.loop(0, count // step)
        def _(i):
            ks = [lo + i * step + e for e in range(step)]
            vs = [outer(r, k) for k in ks]
            for k, v in zip(ks, vs):
                tot[r][k] = tot[r][tab[REL + k, 1]] + v

    def project_part(m, base, part_no):
        lo, count = spans(base, part_no)
        for e in range(count):
            project(m, lo + e)

    def groups(r):
        @pl.loop(0, N // 4)
        def _(i):
            for e in range(4):
                g = i * 4 + e
                grp[r][g] = tot[r][tab[LAST + g, 0]].astype(BF16).reshape(grp[r].shape[1:])

    def rr_copy(r, d, h, q, src):
        if q == 3:
            return rcopy(src.at[d], rr[r].at[d, h, q, d], rr_s.at[r, d], rr_r.at[r, d, spot(3 - h, q)], nbr[d])
        return rcopy(src, rr[r].at[d, h, q], rr_s.at[r, d], rr_r.at[r, d, spot(3 - h, q)], nbr[d])

    def ret_send(r, q):
        for d in (0, 1):
            rr_copy(r, d, 3 - q, q, grp[r].at[((5 + q) * sign[d]) % N]).start()

    def ret_own(r):
        for q in (3, 2, 1):
            ret_send(r, q)

    def ret_raw(r, part_no):
        for h, q in (((0, 3), (1, 2), (2, 1)), ((1, 3), (2, 2)), ((2, 3),))[part_no]:
            for d in (0, 1):
                rr_copy(r, d, h, q, rr[r].at[d, h, q]).wait_recv()
                rr_copy(r, d, h + 1, q, rr[r].at[d, h, q]).start()
        if part_no == 1:
            ret_send(r, 0)

    def rd_copy(r, d, u, s):
        return rcopy(sd[r].at[d, u, s], rd[r].at[d, u, s], rd_s.at[r, d], rd_r.at[r, d, u, s], nbr[d])

    def masked(flag, v):
        return jnp.where(flag, v, jnp.zeros_like(v))

    def ret_combine(r):
        for d in (0, 1):
            for q in (3, 2, 1, 0):
                rr_copy(r, d, 3, q, rr[r].at[d, 3, q]).wait_recv()
            o = at(4 * sign[d])
            for s in range(OWN):
                acc = masked(sel(me, o) == s, grp[r][(4 * sign[d]) % N].astype(F32))
                for q in (0, 1, 2):
                    acc = acc + masked(sel(at(-(q + 1) * sign[d]), o) == s, rr[r][d, 3, q].astype(F32))
                far = masked(sel(at(-4 * sign[d]), o) == s, rr[r][d, 3, 3, d].astype(F32))
                sd[r][d, 0, s, d] = (acc[d] + far).astype(BF16)
                sd[r][d, 0, s, 1 - d] = acc[1 - d].astype(BF16)
                rd_copy(r, d, 0, s).start()

    def ret_dense(r, i):
        u, s = i // OWN, i % OWN
        for d in (0, 1):
            rd_copy(r, d, u, s).wait_recv()
            offset = (3 - u) * sign[d]
            own = grp[r][lax.rem(offset + N, N)].astype(F32)
            v = rd[r][d, u, s].astype(F32) + masked(sel(me, at(offset)) == s, own)
            sd[r][d, u + 1, s] = v.astype(BF16)
            rd_copy(r, d, u + 1, s).start()

    def ret_final(r):
        for s in range(OWN):
            v = masked(sel(me, me) == s, grp[r][0].astype(F32))
            for d in (0, 1):
                rd_copy(r, d, 3, s).wait_recv()
                v = v + rd[r][d, 3, s].astype(F32)
            out[r][s] = v.astype(BF16)

    def loop(lo, hi, f):
        if hi > lo:
            pl.loop(lo, hi)(f)

    copies = (
        pltpu.make_async_copy(c_hbm, cv, local_sem.at[0]),
        pltpu.make_async_copy(x_hbm, xv, local_sem.at[1]),
    )
    for j in range(OWN):
        gather_first(0, j)
    for cp in copies:
        cp.start()
    move = build_tables()
    loop(0, 4, lambda i: gather_dense(0, i))
    for r in (0, 1):
        tot[r][2 * half] = jnp.zeros(tot[r].shape[1:], F32)
    move.wait()
    for cp in copies:
        cp.wait()
    loop(4, 12, lambda i: gather_dense(0, i))
    gather_select(0)
    gather_first(1, 0)
    gather_tail(0, lambda h: gather_first(1, h + 1))
    build(0)
    gather_dense(1, 0)
    project_part(0, theirs, 0)
    gather_dense(1, 1)
    project_part(0, theirs, 1)
    core1(0).start()
    gather_dense(1, 2)
    project_part(0, mine, 0)
    gather_dense(1, 3)
    project_part(0, mine, 1)
    gather_dense(1, 4)
    reduce_start(0)
    loop(5, 10, lambda i: gather_dense(1, i))
    reduce_mid(0)
    loop(10, 12, lambda i: gather_dense(1, i))
    gather_select(1)
    reduce_end(0)

    def fill(h):
        if h == 0:
            outer_part(0, mine, 0)
            outer_part(0, mine, 1)
            core2(0, theirs).wait_recv()
        else:
            outer_part(0, theirs, h - 1)

    gather_tail(1, fill)
    groups(0)
    ret_own(0)
    build(1)
    project_part(1, theirs, 0)
    project_part(1, theirs, 1)
    core1(1).start()
    project_part(1, mine, 0)
    project_part(1, mine, 1)
    ret_raw(0, 0)
    ret_raw(0, 1)
    reduce_start(1)
    ret_raw(0, 2)
    ret_combine(0)
    loop(0, 3, lambda i: ret_dense(0, i))
    reduce_mid(1)
    loop(3, 8, lambda i: ret_dense(0, i))
    reduce_end(1)
    outer_part(1, mine, 0)
    outer_part(1, mine, 1)
    loop(8, 10, lambda i: ret_dense(0, i))
    core2(1, theirs).wait_recv()
    outer_part(1, theirs, 0)
    loop(10, 11, lambda i: ret_dense(0, i))
    outer_part(1, theirs, 1)
    loop(11, 12, lambda i: ret_dense(0, i))
    groups(1)
    ret_own(1)
    for h in range(3):
        ret_raw(1, h)
    ret_combine(1)
    ret_final(0)
    loop(0, 12, lambda i: ret_dense(1, i))
    ret_final(1)

    for m in (0, 1):
        core1(m).wait_send()
        core2(m, mine).wait_send()
        if chips > 1:
            pieces_of(m, rs_s, rs_r).wait_send()
            pieces_of(m, ag_s, ag_r).wait_send()
        for d in (0, 1):
            for buf, sem in ((gd, gd_s), (rd, rd_s)):
                rcopy(buf[m].at[d], buf[m].at[d], sem.at[m, d], sem.at[m, d], nbr[d]).wait_send()
            for buf, sem in ((gs, gs_s), (rr, rr_s)):
                span = buf[m].at[d, pl.ds(0, 2)]
                rcopy(span, span, sem.at[m, d], sem.at[m, d], nbr[d]).wait_send()


def finish(a_ref, b_ref, oa_ref, ob_ref):
    oa_ref[...] = a_ref[...]
    ob_ref[...] = b_ref[...]


def body(chips, inputs, cotangent, factor_a, factor_b, adapter_slot, seg_adapter):
    segs = seg_adapter.shape[1]
    rows = inputs.shape[0] // segs
    feat = inputs.shape[1]
    per = -(-segs // (2 * chips))
    half = chips * per
    a_unit, b_unit = (2, feat // 2, 128), (2, 64, feat)
    bf = lambda *shape: pltpu.VMEM(shape, BF16)
    fl = lambda *shape: pltpu.VMEM(shape, F32)
    dma = lambda *shape: pltpu.SemaphoreType.DMA(shape)
    vm = pl.BlockSpec(memory_space=pltpu.VMEM)
    scratch = [
        bf(segs, rows, feat), bf(segs, rows, feat),
        bf(2, 4, 4, *a_unit), bf(2, 4, 4, *b_unit),
        bf(2, 4, 4, *a_unit), bf(2, 4, 4, *b_unit),
        bf(2, 4, *a_unit), bf(2, 4, *b_unit),
        bf(N, *a_unit), bf(N, *b_unit),
        fl(2, 2 * half, rows, 128), fl(2, half, rows, 128), bf(2, half, rows, 128),
        bf(2, chips, per, rows, 128), bf(2, 2 * half, rows, 128),
        fl(2 * half + 1, feat, 128), fl(2 * half + 1, 128, feat),
        bf(N, *a_unit), bf(N, *b_unit),
        bf(2, 4, 4, *a_unit), bf(2, 4, 4, *b_unit),
        bf(2, 4, 4, *a_unit), bf(2, 4, 4, *b_unit),
        bf(2, 4, 4, *a_unit), bf(2, 4, 4, *b_unit),
        pltpu.VMEM((64, 128), jnp.int32), pltpu.SMEM((64, 128), jnp.int32),
        dma(3),
        dma(2, 2), dma(2, 2, 4, 4), dma(2, 2), dma(2, 2, 10),
        dma(2, 2), dma(2, 2, 10), dma(2, 2), dma(2, 2, 4, 4),
    ] + [dma(2)] * 8
    grad_a, grad_b = pl.pallas_call(
        functools.partial(kernel, segs, chips, per),
        out_shape=(
            jax.ShapeDtypeStruct((OWN,) + a_unit, BF16),
            jax.ShapeDtypeStruct((OWN,) + b_unit, BF16),
        ),
        in_specs=[
            pl.BlockSpec(memory_space=pltpu.SMEM),
            vm,
            pl.BlockSpec(memory_space=pl.ANY),
            pl.BlockSpec(memory_space=pl.ANY),
            vm, vm,
        ],
        out_specs=(vm, vm),
        scratch_shapes=scratch,
        compiler_params=pltpu.CompilerParams(
            collective_id=0, has_side_effects=True, vmem_limit_bytes=60 << 20
        ),
        name="adapter_backward",
    )(
        adapter_slot,
        seg_adapter,
        inputs.reshape(segs, rows, feat),
        cotangent.reshape(segs, rows, feat),
        factor_a.reshape((OWN,) + a_unit),
        factor_b.reshape((OWN,) + b_unit),
    )
    grad_a, grad_b = pl.pallas_call(
        finish,
        out_shape=(jax.ShapeDtypeStruct(grad_a.shape, BF16), jax.ShapeDtypeStruct(grad_b.shape, BF16)),
        in_specs=[vm, vm],
        out_specs=(vm, vm),
        name="finish",
    )(grad_a, grad_b)
    return grad_a.reshape(factor_a.shape), grad_b.reshape(factor_b.shape)


def solution(mesh):
    return jax.shard_map(
        functools.partial(body, mesh.shape["tp"] // 2),
        mesh=mesh,
        in_specs=(
            P("grp", "tp"),
            P("grp", "tp"),
            P("grp", "tp", None),
            P("grp", None, "tp"),
            P(),
            P(),
        ),
        out_specs=(P("grp", "tp", None), P("grp", None, "tp")),
        check_vma=False,
    )
```

```python
import functools
import math

import jax
import jax.numpy as jnp
from jax import lax
from jax.experimental import pallas as pl
from jax.experimental.pallas import tpu as pltpu
from jax.sharding import PartitionSpec as P

MESH = pl.DeviceIdType.MESH
N = 16
OWN = 4
F32 = jnp.float32
BF16 = jnp.bfloat16
REL, LAST = 16, 48


def kernel(
    segs, chips, per,
    slot_hbm, seg_hbm, x_hbm, c_hbm, a_hbm, b_hbm,
    oa, ob,
    xv, cv, fa, fb, aslot, seg,
    gda, gdb, gsa, gsb, ssa, ssb, wa, wb,
    part, other, pair, pieces, low,
    ta, tb, ga, gb,
    rra, rrb, rda, rdb, sda, sdb,
    vtab, tab,
    local_sem, gd_s, gd_r, gs_s, gs_r, rr_s, rr_r, rd_s, rd_r,
    c1_s, c1_r, rs_s, rs_r, ag_s, ag_r, c2_s, c2_r,
):
    me = lax.axis_index("grp")
    tp = lax.axis_index("tp")
    chip = tp // 2
    core = tp % 2
    half = chips * per
    mine = core * half
    theirs = (1 - core) * half
    up = {"grp": lax.rem(me + 1, N), "tp": tp}
    down = {"grp": lax.rem(me + N - 1, N), "tp": tp}
    nbr = (up, down)
    sib = {"grp": me, "tp": chip * 2 + 1 - core}

    side = math.isqrt(chips)

    def hops(step):
        return sum(min(e, side - e) for e in divmod(step, side))

    others = sorted(range(1, chips), key=lambda step: -hops(step))

    def chip_at(step):
        dy, dx = divmod(step, side)
        return lax.rem(chip // side + dy, side) * side + lax.rem(chip % side + dx, side)

    def chip_dev(step):
        return {"grp": me, "tp": chip_at(step) * 2 + core}

    def rcopy(src, dst, ss, rs, dev):
        return pltpu.make_async_remote_copy(
            src_ref=src, dst_ref=dst, send_sem=ss, recv_sem=rs,
            device_id=dev, device_id_type=MESH,
        )

    fac, gd, gs, ss, w, tok = (fb, fa), (gdb, gda), (gsb, gsa), (ssb, ssa), (wb, wa), (cv, xv)
    tot, grp, rr, rd, sd, out = (ta, tb), (ga, gb), (rra, rrb), (rda, rdb), (sda, sdb), (oa, ob)
    sign = (1, -1)

    def at(offset):
        return lax.rem(me + offset + 2 * N, N)

    def sel(g, o):
        return tab[g, o]

    barrier = pltpu.get_barrier_semaphore()
    for dev in (up, down, sib):
        pl.semaphore_signal(barrier, inc=1, device_id=dev, device_id_type=MESH)
    for p in others:
        pl.semaphore_signal(barrier, inc=1, device_id=chip_dev(p), device_id_type=MESH)
    copies = [
        pltpu.make_async_copy(src, dst, local_sem.at[i])
        for i, (src, dst) in enumerate((
            (slot_hbm, aslot), (seg_hbm, seg), (b_hbm, fb), (a_hbm, fa), (c_hbm, cv), (x_hbm, xv),
        ))
    ]
    for cp in copies:
        cp.start()
    pl.semaphore_wait(barrier, 3 + chips - 1)

    def build_tables():
        ids = seg[...]
        zero = jnp.zeros_like(ids)
        slot = lax.fori_loop(0, aslot.shape[0], lambda n, a: jnp.where(ids == n, aslot[n], a), zero)
        owner, place = lax.shift_right_logical(slot, 2), slot & 3

        def iota(rows, cols, dim):
            return lax.broadcasted_iota(jnp.int32, (rows, cols), dim)

        lane = iota(N, 128, 1)
        chosen = jnp.zeros((N, 128), jnp.int32)
        for o in range(N):
            best = jnp.max(jnp.where(owner == o, place, 0), axis=1, keepdims=True)
            chosen = jnp.where(lane == o, best, chosen)
        vtab[0:N] = chosen
        row = jnp.sum(jnp.where(iota(N, segs, 0) == me, owner, 0), axis=0, keepdims=True)
        row = (row - me + N) & (N - 1)
        wide = jnp.broadcast_to(row, (32, segs))
        down32, right32 = iota(32, segs, 0), iota(32, segs, 1)
        col = jnp.sum(jnp.where(down32 == right32, wide, 0), axis=1, keepdims=True)
        size = 2 * half

        def turn(k):
            return jnp.where(k >= mine, k - mine, k - mine + size)

        def back(best):
            k = best + mine
            return jnp.where(best < 0, size, jnp.where(k >= size, k - size, k))

        right_turn, down_turn = turn(right32), turn(down32)
        prev = back(jnp.max(
            jnp.where((wide == col) & (right_turn < down_turn), right_turn, -1), axis=1, keepdims=True
        ))
        vtab[REL:REL + 32] = jnp.where(iota(32, 128, 1) == 0, col, prev)
        last = back(jnp.max(
            jnp.where(wide[0:N] == iota(N, segs, 0), right_turn[0:N], -1), axis=1, keepdims=True
        ))
        vtab[LAST:LAST + N] = jnp.broadcast_to(last, (N, 128))
        move = pltpu.make_async_copy(vtab, tab, local_sem.at[6])
        move.start()
        return move

    def spot(h, q):
        return (0, 4, 7, 9)[h] + q - h

    def gd_copy(m, d, t, j, src):
        return rcopy(src, gd[m].at[d, t, j], gd_s.at[m, d], gd_r.at[m, d, t, j], nbr[d])

    def gather_first(m, j):
        for d in (0, 1):
            gd_copy(m, d, 0, j, fac[m].at[j]).start()

    def gather_dense(m, i):
        t, j = i // OWN, i % OWN
        for d in (0, 1):
            gd_copy(m, d, t, j, gd[m].at[d, t, j]).wait_recv()
            gd_copy(m, d, t + 1, j, gd[m].at[d, t, j]).start()

    def gs_copy(m, d, h, q, src):
        if q == 3:
            return rcopy(src.at[d], gs[m].at[d, h, q, d], gs_s.at[m, d], gs_r.at[m, d, spot(h, q)], nbr[d])
        return rcopy(src, gs[m].at[d, h, q], gs_s.at[m, d], gs_r.at[m, d, spot(h, q)], nbr[d])

    def pick(ref4, s):
        a = jnp.where(s == 0, ref4[0], ref4[1])
        b = jnp.where(s == 2, ref4[2], ref4[3])
        return jnp.where(s < 2, a, b)

    def gather_select(m):
        for d in (0, 1):
            for j in range(OWN):
                gd_copy(m, d, 3, j, gd[m].at[d, 3, j]).wait_recv()
        for q in (3, 2, 1, 0):
            for d in (0, 1):
                o = at(-4 * sign[d])
                s = sel(at((q + 1) * sign[d]), o)
                ss[m][d, q] = pick(gd[m].at[d, 3], s)
                gs_copy(m, d, 0, q, ss[m].at[d, q]).start()

    def gather_tail(m, filler):
        for h in range(3):
            for q in range(3, h, -1):
                for d in (0, 1):
                    gs_copy(m, d, h, q, gs[m].at[d, h, q]).wait_recv()
                    gs_copy(m, d, h + 1, q, gs[m].at[d, h, q]).start()
            filler(h)
        for h in range(4):
            for d in (0, 1):
                gs_copy(m, d, h, h, gs[m].at[d, h, h]).wait_recv()

    def build(m):
        w[m][0] = pick(fac[m], sel(me, me))
        for d in (0, 1):
            for t in range(1, 5):
                w[m][(-t * sign[d]) % N] = pick(gd[m].at[d, t - 1], sel(me, at(-t * sign[d])))
            for h in range(3):
                w[m][(-(5 + h) * sign[d]) % N] = gs[m][d, h, h]
            w[m][8, d] = gs[m][d, 3, 3, d]

    def project(m, k):
        rows = tok[m][jnp.minimum(k, segs - 1)]
        rel = tab[REL + k, 0]
        if m == 0:
            f = w[m][rel].reshape(128, rows.shape[1])
            v = lax.dot_general(rows, f, (((1,), (1,)), ((), ())), preferred_element_type=F32)
        else:
            f = w[m][rel].reshape(rows.shape[1], 128)
            v = lax.dot_general(rows, f, (((1,), (0,)), ((), ())), preferred_element_type=F32)
        part[m, k] = v

    def core1(m):
        return rcopy(part.at[m, pl.ds(theirs, half)], other.at[m], c1_s.at[m], c1_r.at[m], sib)

    def rs_copy(m, p):
        dest = chip_at(p)
        return rcopy(pair.at[m, pl.ds(dest * per, per)], pieces.at[m, p], rs_s.at[m], rs_r.at[m], chip_dev(p))

    def ag_copy(m, p):
        spot = low.at[m, pl.ds(mine + chip * per, per)]
        return rcopy(spot, spot, ag_s.at[m], ag_r.at[m], chip_dev(p))

    def core2(m, base):
        spot = low.at[m, pl.ds(base, half)]
        return rcopy(spot, spot, c2_s.at[m], c2_r.at[m], sib)

    def reduce_start(m):
        core1(m).wait_recv()

        @pl.loop(0, half)
        def _(h):
            pair[m, h] = (part[m, mine + h] + other[m, h]).astype(BF16)

        for p in others:
            rs_copy(m, p).start()

    def pieces_of(m, ss, rs):
        span = pieces.at[m, pl.ds(1, chips - 1)]
        return rcopy(span, span, ss.at[m], rs.at[m], sib)

    def reduce_mid(m):
        if chips > 1:
            pieces_of(m, rs_s, rs_r).wait_recv()
        for l in range(per):
            acc = pair[m, chip * per + l].astype(F32)
            if chips > 1:
                acc = lax.fori_loop(1, chips, lambda p, a: a + pieces[m, p, l].astype(F32), acc)
            low[m, mine + chip * per + l] = acc.astype(BF16)
        for p in others:
            ag_copy(m, p).start()

    def reduce_end(m):
        if chips > 1:
            pieces_of(m, ag_s, ag_r).wait_recv()
        core2(m, mine).start()

    def outer(r, k):
        if r == 0:
            return lax.dot_general(xv[jnp.minimum(k, segs - 1)], low[0, k], (((0,), (0,)), ((), ())), preferred_element_type=F32)
        return lax.dot_general(low[1, k], cv[jnp.minimum(k, segs - 1)], (((0,), (0,)), ((), ())), preferred_element_type=F32)

    quarter = -(-half // 2)
    step = 4 if half % 8 == 0 else 1

    def spans(base, part_no):
        return base + part_no * quarter, min(quarter, half - part_no * quarter)

    def outer_part(r, base, part_no):
        lo, count = spans(base, part_no)

        @pl.loop(0, count // step)
        def _(i):
            ks = [lo + i * step + e for e in range(step)]
            vs = [outer(r, k) for k in ks]
            for k, v in zip(ks, vs):
                tot[r][k] = tot[r][tab[REL + k, 1]] + v

    def project_part(m, base, part_no):
        lo, count = spans(base, part_no)
        for e in range(count):
            project(m, lo + e)

    def groups(r):
        @pl.loop(0, N // 4)
        def _(i):
            for e in range(4):
                g = i * 4 + e
                grp[r][g] = tot[r][tab[LAST + g, 0]].astype(BF16).reshape(grp[r].shape[1:])

    def rr_copy(r, d, h, q, src):
        if q == 3:
            return rcopy(src.at[d], rr[r].at[d, h, q, d], rr_s.at[r, d], rr_r.at[r, d, spot(3 - h, q)], nbr[d])
        return rcopy(src, rr[r].at[d, h, q], rr_s.at[r, d], rr_r.at[r, d, spot(3 - h, q)], nbr[d])

    def ret_send(r, q):
        for d in (0, 1):
            rr_copy(r, d, 3 - q, q, grp[r].at[((5 + q) * sign[d]) % N]).start()

    def ret_own(r):
        for q in (3, 2, 1):
            ret_send(r, q)

    def ret_raw(r, part_no):
        for h, q in (((0, 3), (1, 2), (2, 1)), ((1, 3), (2, 2)), ((2, 3),))[part_no]:
            for d in (0, 1):
                rr_copy(r, d, h, q, rr[r].at[d, h, q]).wait_recv()
                rr_copy(r, d, h + 1, q, rr[r].at[d, h, q]).start()
        if part_no == 1:
            ret_send(r, 0)

    def rd_copy(r, d, u, s):
        return rcopy(sd[r].at[d, u, s], rd[r].at[d, u, s], rd_s.at[r, d], rd_r.at[r, d, u, s], nbr[d])

    def masked(flag, v):
        return jnp.where(flag, v, jnp.zeros_like(v))

    def ret_combine(r):
        for d in (0, 1):
            for q in (3, 2, 1, 0):
                rr_copy(r, d, 3, q, rr[r].at[d, 3, q]).wait_recv()
        for s in range(OWN):
            for d in (0, 1):
                o = at(4 * sign[d])
                acc = masked(sel(me, o) == s, grp[r][(4 * sign[d]) % N].astype(F32))
                for q in (0, 1, 2):
                    acc = acc + masked(sel(at(-(q + 1) * sign[d]), o) == s, rr[r][d, 3, q].astype(F32))
                far = masked(sel(at(-4 * sign[d]), o) == s, rr[r][d, 3, 3, d].astype(F32))
                sd[r][d, 0, s, d] = (acc[d] + far).astype(BF16)
                sd[r][d, 0, s, 1 - d] = acc[1 - d].astype(BF16)
                rd_copy(r, d, 0, s).start()

    def ret_dense(r, i):
        u, s = i // OWN, i % OWN
        for d in (0, 1):
            rd_copy(r, d, u, s).wait_recv()
            offset = (3 - u) * sign[d]
            own = grp[r][lax.rem(offset + N, N)].astype(F32)
            v = rd[r][d, u, s].astype(F32) + masked(sel(me, at(offset)) == s, own)
            sd[r][d, u + 1, s] = v.astype(BF16)
            rd_copy(r, d, u + 1, s).start()

    def ret_final(r):
        for s in range(OWN):
            v = masked(sel(me, me) == s, grp[r][0].astype(F32))
            for d in (0, 1):
                rd_copy(r, d, 3, s).wait_recv()
                v = v + rd[r][d, 3, s].astype(F32)
            out[r][s] = v.astype(BF16)

    def loop(lo, hi, f):
        if hi > lo:
            pl.loop(lo, hi)(f)

    copies[2].wait()
    for j in range(OWN):
        gather_first(0, j)
    copies[0].wait()
    copies[1].wait()
    move = build_tables()
    loop(0, 4, lambda i: gather_dense(0, i))
    for r in (0, 1):
        tot[r][2 * half] = jnp.zeros(tot[r].shape[1:], F32)
    move.wait()
    for cp in copies[3:]:
        cp.wait()
    loop(4, 12, lambda i: gather_dense(0, i))
    gather_select(0)
    gather_first(1, 0)
    gather_tail(0, lambda h: gather_first(1, h + 1))
    build(0)
    gather_dense(1, 0)
    project_part(0, theirs, 0)
    gather_dense(1, 1)
    project_part(0, theirs, 1)
    core1(0).start()
    gather_dense(1, 2)
    project_part(0, mine, 0)
    gather_dense(1, 3)
    project_part(0, mine, 1)
    gather_dense(1, 4)
    reduce_start(0)
    loop(5, 10, lambda i: gather_dense(1, i))
    reduce_mid(0)
    loop(10, 12, lambda i: gather_dense(1, i))
    gather_select(1)
    reduce_end(0)

    def fill(h):
        if h == 0:
            outer_part(0, mine, 0)
            outer_part(0, mine, 1)
            core2(0, theirs).wait_recv()
            outer_part(0, theirs, 0)
        elif h == 1:
            outer_part(0, theirs, 1)
            groups(0)
        else:
            ret_own(0)

    gather_tail(1, fill)
    build(1)
    project_part(1, theirs, 0)
    project_part(1, theirs, 1)
    core1(1).start()
    project_part(1, mine, 0)
    project_part(1, mine, 1)
    ret_raw(0, 0)
    ret_raw(0, 1)
    reduce_start(1)
    ret_raw(0, 2)
    ret_combine(0)
    loop(0, 4, lambda i: ret_dense(0, i))
    reduce_mid(1)
    loop(4, 9, lambda i: ret_dense(0, i))
    reduce_end(1)
    outer_part(1, mine, 0)
    outer_part(1, mine, 1)
    loop(9, 11, lambda i: ret_dense(0, i))
    core2(1, theirs).wait_recv()
    outer_part(1, theirs, 0)
    ret_dense(0, 11)
    outer_part(1, theirs, 1)
    groups(1)
    ret_own(1)
    for h in range(3):
        ret_raw(1, h)
    ret_combine(1)
    ret_final(0)
    loop(0, 12, lambda i: ret_dense(1, i))
    ret_final(1)

    for m in (0, 1):
        core1(m).wait_send()
        core2(m, mine).wait_send()
        if chips > 1:
            pieces_of(m, rs_s, rs_r).wait_send()
            pieces_of(m, ag_s, ag_r).wait_send()
        for d in (0, 1):
            for buf, sem in ((gd, gd_s), (rd, rd_s)):
                rcopy(buf[m].at[d], buf[m].at[d], sem.at[m, d], sem.at[m, d], nbr[d]).wait_send()
            for buf, sem in ((gs, gs_s), (rr, rr_s)):
                span = buf[m].at[d, pl.ds(0, 2)]
                rcopy(span, span, sem.at[m, d], sem.at[m, d], nbr[d]).wait_send()


def finish(a_ref, b_ref, oa_ref, ob_ref):
    oa_ref[...] = a_ref[...]
    ob_ref[...] = b_ref[...]


def body(chips, inputs, cotangent, factor_a, factor_b, adapter_slot, seg_adapter):
    segs = seg_adapter.shape[1]
    rows = inputs.shape[0] // segs
    feat = inputs.shape[1]
    per = -(-segs // (2 * chips))
    half = chips * per
    a_unit, b_unit = (2, feat // 2, 128), (2, 64, feat)
    bf = lambda *shape: pltpu.VMEM(shape, BF16)
    fl = lambda *shape: pltpu.VMEM(shape, F32)
    dma = lambda *shape: pltpu.SemaphoreType.DMA(shape)
    vm = pl.BlockSpec(memory_space=pltpu.VMEM)
    scratch = [
        bf(segs, rows, feat), bf(segs, rows, feat), bf(OWN, *a_unit), bf(OWN, *b_unit),
        pltpu.SMEM(adapter_slot.shape, jnp.int32), pltpu.VMEM(seg_adapter.shape, jnp.int32),
        bf(2, 4, 4, *a_unit), bf(2, 4, 4, *b_unit),
        bf(2, 4, 4, *a_unit), bf(2, 4, 4, *b_unit),
        bf(2, 4, *a_unit), bf(2, 4, *b_unit),
        bf(N, *a_unit), bf(N, *b_unit),
        fl(2, 2 * half, rows, 128), fl(2, half, rows, 128), bf(2, half, rows, 128),
        bf(2, chips, per, rows, 128), bf(2, 2 * half, rows, 128),
        fl(2 * half + 1, feat, 128), fl(2 * half + 1, 128, feat),
        bf(N, *a_unit), bf(N, *b_unit),
        bf(2, 4, 4, *a_unit), bf(2, 4, 4, *b_unit),
        bf(2, 4, 4, *a_unit), bf(2, 4, 4, *b_unit),
        bf(2, 4, 4, *a_unit), bf(2, 4, 4, *b_unit),
        pltpu.VMEM((64, 128), jnp.int32), pltpu.SMEM((64, 128), jnp.int32),
        dma(7),
        dma(2, 2), dma(2, 2, 4, 4), dma(2, 2), dma(2, 2, 10),
        dma(2, 2), dma(2, 2, 10), dma(2, 2), dma(2, 2, 4, 4),
    ] + [dma(2)] * 8
    grad_a, grad_b = pl.pallas_call(
        functools.partial(kernel, segs, chips, per),
        out_shape=(
            jax.ShapeDtypeStruct((OWN,) + a_unit, BF16),
            jax.ShapeDtypeStruct((OWN,) + b_unit, BF16),
        ),
        in_specs=[
            pl.BlockSpec(memory_space=pl.ANY),
        ] * 6,
        out_specs=(vm, vm),
        scratch_shapes=scratch,
        compiler_params=pltpu.CompilerParams(
            collective_id=0, has_side_effects=True, vmem_limit_bytes=60 << 20
        ),
        name="adapter_backward",
    )(
        adapter_slot,
        seg_adapter,
        inputs.reshape(segs, rows, feat),
        cotangent.reshape(segs, rows, feat),
        factor_a.reshape((OWN,) + a_unit),
        factor_b.reshape((OWN,) + b_unit),
    )
    grad_a, grad_b = pl.pallas_call(
        finish,
        out_shape=(jax.ShapeDtypeStruct(grad_a.shape, BF16), jax.ShapeDtypeStruct(grad_b.shape, BF16)),
        in_specs=[vm, vm],
        out_specs=(vm, vm),
        name="finish",
    )(grad_a, grad_b)
    return grad_a.reshape(factor_a.shape), grad_b.reshape(factor_b.shape)


def solution(mesh):
    return jax.shard_map(
        functools.partial(body, mesh.shape["tp"] // 2),
        mesh=mesh,
        in_specs=(
            P("grp", "tp"),
            P("grp", "tp"),
            P("grp", "tp", None),
            P("grp", None, "tp"),
            P(),
            P(),
        ),
        out_specs=(P("grp", "tp", None), P("grp", None, "tp")),
        check_vma=False,
    )
```

```python
import functools
import math

import jax
import jax.numpy as jnp
from jax import lax
from jax.experimental import pallas as pl
from jax.experimental.pallas import tpu as pltpu
from jax.sharding import PartitionSpec as P

MESH = pl.DeviceIdType.MESH
N = 16
OWN = 4
F32 = jnp.float32
BF16 = jnp.bfloat16
REL, LAST = 16, 48


def kernel(
    segs, chips, per,
    slot_hbm, seg_hbm, x_hbm, c_hbm, a_hbm, b_hbm,
    oa, ob,
    xv, cv, fa, fb, aslot, seg,
    gda, gdb, gsa, gsb, ssa, ssb, wa, wb,
    part, other, pair, pieces, low,
    ta, tb, ga, gb,
    rra, rrb, rda, rdb, sda, sdb,
    vtab, tab,
    local_sem, gd_s, gd_r, gs_s, gs_r, rr_s, rd_s,
    c1_s, c1_r, rs_s, rs_r, ag_s, ag_r, c2_s, c2_r,
):
    me = lax.axis_index("grp")
    tp = lax.axis_index("tp")
    chip = tp // 2
    core = tp % 2
    half = chips * per
    mine = core * half
    theirs = (1 - core) * half
    up = {"grp": lax.rem(me + 1, N), "tp": tp}
    down = {"grp": lax.rem(me + N - 1, N), "tp": tp}
    nbr = (up, down)
    sib = {"grp": me, "tp": chip * 2 + 1 - core}

    side = math.isqrt(chips)

    def hops(step):
        return sum(min(e, side - e) for e in divmod(step, side))

    others = sorted(range(1, chips), key=lambda step: -hops(step))

    def chip_at(step):
        dy, dx = divmod(step, side)
        return lax.rem(chip // side + dy, side) * side + lax.rem(chip % side + dx, side)

    def chip_dev(step):
        return {"grp": me, "tp": chip_at(step) * 2 + core}

    def rcopy(src, dst, ss, rs, dev):
        return pltpu.make_async_remote_copy(
            src_ref=src, dst_ref=dst, send_sem=ss, recv_sem=rs,
            device_id=dev, device_id_type=MESH,
        )

    fac, gd, gs, ss, w, tok = (fb, fa), (gdb, gda), (gsb, gsa), (ssb, ssa), (wb, wa), (cv, xv)
    tot, grp, rr, rd, sd, out = (ta, tb), (ga, gb), (rra, rrb), (rda, rdb), (sda, sdb), (oa, ob)
    sign = (1, -1)
    rd_r, rr_r = gd_r, gs_r

    def at(offset):
        return lax.rem(me + offset + 2 * N, N)

    def sel(g, o):
        return tab[g, o]

    barrier = pltpu.get_barrier_semaphore()
    for dev in (up, down, sib):
        pl.semaphore_signal(barrier, inc=1, device_id=dev, device_id_type=MESH)
    for p in others:
        pl.semaphore_signal(barrier, inc=1, device_id=chip_dev(p), device_id_type=MESH)
    copies = [
        pltpu.make_async_copy(src, dst, local_sem.at[i])
        for i, (src, dst) in enumerate((
            (slot_hbm, aslot), (seg_hbm, seg), (b_hbm, fb), (a_hbm, fa), (c_hbm, cv), (x_hbm, xv),
        ))
    ]
    for cp in copies:
        cp.start()
    pl.semaphore_wait(barrier, 3 + chips - 1)

    def build_tables():
        ids = seg[...]
        zero = jnp.zeros_like(ids)
        slot = lax.fori_loop(0, aslot.shape[0], lambda n, a: jnp.where(ids == n, aslot[n], a), zero)
        owner, place = lax.shift_right_logical(slot, 2), slot & 3

        def iota(rows, cols, dim):
            return lax.broadcasted_iota(jnp.int32, (rows, cols), dim)

        lane = iota(N, 128, 1)
        chosen = jnp.zeros((N, 128), jnp.int32)
        for o in range(N):
            best = jnp.max(jnp.where(owner == o, place, 0), axis=1, keepdims=True)
            chosen = jnp.where(lane == o, best, chosen)
        vtab[0:N] = chosen
        row = jnp.sum(jnp.where(iota(N, segs, 0) == me, owner, 0), axis=0, keepdims=True)
        row = (row - me + N) & (N - 1)
        wide = jnp.broadcast_to(row, (32, segs))
        down32, right32 = iota(32, segs, 0), iota(32, segs, 1)
        col = jnp.sum(jnp.where(down32 == right32, wide, 0), axis=1, keepdims=True)
        size = 2 * half

        def turn(k):
            return jnp.where(k >= mine, k - mine, k - mine + size)

        def back(best):
            k = best + mine
            return jnp.where(best < 0, size, jnp.where(k >= size, k - size, k))

        right_turn, down_turn = turn(right32), turn(down32)
        prev = back(jnp.max(
            jnp.where((wide == col) & (right_turn < down_turn), right_turn, -1), axis=1, keepdims=True
        ))
        vtab[REL:REL + 32] = jnp.where(iota(32, 128, 1) == 0, col, prev)
        last = back(jnp.max(
            jnp.where(wide[0:N] == iota(N, segs, 0), right_turn[0:N], -1), axis=1, keepdims=True
        ))
        vtab[LAST:LAST + N] = jnp.broadcast_to(last, (N, 128))
        move = pltpu.make_async_copy(vtab, tab, local_sem.at[6])
        move.start()
        return move

    def spot(h, q):
        return (0, 4, 7, 9)[h] + q - h

    def gd_copy(m, d, t, j, src):
        return rcopy(src, gd[m].at[d, t, j], gd_s.at[m, d], gd_r.at[m, d, t, j], nbr[d])

    def gather_first(m, j):
        for d in (0, 1):
            gd_copy(m, d, 0, j, fac[m].at[j]).start()

    def gather_dense(m, i):
        t, j = i // OWN, i % OWN
        for d in (0, 1):
            gd_copy(m, d, t, j, gd[m].at[d, t, j]).wait_recv()
            gd_copy(m, d, t + 1, j, gd[m].at[d, t, j]).start()

    def gs_copy(m, d, h, q, src):
        if q == 3:
            return rcopy(src.at[d], gs[m].at[d, h, q, d], gs_s.at[m, d], gs_r.at[m, d, spot(h, q)], nbr[d])
        return rcopy(src, gs[m].at[d, h, q], gs_s.at[m, d], gs_r.at[m, d, spot(h, q)], nbr[d])

    def pick(ref4, s):
        a = jnp.where(s == 0, ref4[0], ref4[1])
        b = jnp.where(s == 2, ref4[2], ref4[3])
        return jnp.where(s < 2, a, b)

    def gather_select(m):
        for d in (0, 1):
            for j in range(OWN):
                gd_copy(m, d, 3, j, gd[m].at[d, 3, j]).wait_recv()
        for q in (3, 2, 1, 0):
            for d in (0, 1):
                o = at(-4 * sign[d])
                s = sel(at((q + 1) * sign[d]), o)
                ss[m][d, q] = pick(gd[m].at[d, 3], s)
                gs_copy(m, d, 0, q, ss[m].at[d, q]).start()

    def gather_tail(m, filler):
        for h in range(3):
            for q in range(3, h, -1):
                for d in (0, 1):
                    gs_copy(m, d, h, q, gs[m].at[d, h, q]).wait_recv()
                    gs_copy(m, d, h + 1, q, gs[m].at[d, h, q]).start()
            filler(h)
        for h in range(4):
            for d in (0, 1):
                gs_copy(m, d, h, h, gs[m].at[d, h, h]).wait_recv()

    def build(m):
        w[m][0] = pick(fac[m], sel(me, me))
        for d in (0, 1):
            for t in range(1, 5):
                w[m][(-t * sign[d]) % N] = pick(gd[m].at[d, t - 1], sel(me, at(-t * sign[d])))
            for h in range(3):
                w[m][(-(5 + h) * sign[d]) % N] = gs[m][d, h, h]
            w[m][8, d] = gs[m][d, 3, 3, d]

    def project(m, k):
        rows = tok[m][jnp.minimum(k, segs - 1)]
        rel = tab[REL + k, 0]
        if m == 0:
            f = w[m][rel].reshape(128, rows.shape[1])
            v = lax.dot_general(rows, f, (((1,), (1,)), ((), ())), preferred_element_type=F32)
        else:
            f = w[m][rel].reshape(rows.shape[1], 128)
            v = lax.dot_general(rows, f, (((1,), (0,)), ((), ())), preferred_element_type=F32)
        part[m, k] = v

    def core1(m):
        return rcopy(part.at[m, pl.ds(theirs, half)], other.at[m], c1_s.at[m], c1_r.at[m], sib)

    def rs_copy(m, p):
        dest = chip_at(p)
        return rcopy(pair.at[m, pl.ds(dest * per, per)], pieces.at[m, p], rs_s.at[m], rs_r.at[m], chip_dev(p))

    def ag_copy(m, p):
        spot = low.at[m, pl.ds(mine + chip * per, per)]
        return rcopy(spot, spot, ag_s.at[m], ag_r.at[m], chip_dev(p))

    def core2(m, base):
        spot = low.at[m, pl.ds(base, half)]
        return rcopy(spot, spot, c2_s.at[m], c2_r.at[m], sib)

    def reduce_start(m):
        core1(m).wait_recv()

        @pl.loop(0, half)
        def _(h):
            pair[m, h] = (part[m, mine + h] + other[m, h]).astype(BF16)

        for p in others:
            rs_copy(m, p).start()

    def pieces_of(m, ss, rs):
        span = pieces.at[m, pl.ds(1, chips - 1)]
        return rcopy(span, span, ss.at[m], rs.at[m], sib)

    def reduce_mid(m):
        if chips > 1:
            pieces_of(m, rs_s, rs_r).wait_recv()
        for l in range(per):
            acc = pair[m, chip * per + l].astype(F32)
            if chips > 1:
                acc = lax.fori_loop(1, chips, lambda p, a: a + pieces[m, p, l].astype(F32), acc)
            low[m, mine + chip * per + l] = acc.astype(BF16)
        for p in others:
            ag_copy(m, p).start()

    def reduce_end(m):
        if chips > 1:
            pieces_of(m, ag_s, ag_r).wait_recv()
        core2(m, mine).start()

    def outer(r, k):
        if r == 0:
            return lax.dot_general(xv[jnp.minimum(k, segs - 1)], low[0, k], (((0,), (0,)), ((), ())), preferred_element_type=F32)
        return lax.dot_general(low[1, k], cv[jnp.minimum(k, segs - 1)], (((0,), (0,)), ((), ())), preferred_element_type=F32)

    quarter = -(-half // 2)
    step = 4 if half % 8 == 0 else 1

    def spans(base, part_no):
        return base + part_no * quarter, min(quarter, half - part_no * quarter)

    def outer_part(r, base, part_no):
        lo, count = spans(base, part_no)

        @pl.loop(0, count // step)
        def _(i):
            ks = [lo + i * step + e for e in range(step)]
            vs = [outer(r, k) for k in ks]
            for k, v in zip(ks, vs):
                tot[r][k] = tot[r][tab[REL + k, 1]] + v

    def project_part(m, base, part_no):
        lo, count = spans(base, part_no)
        for e in range(count):
            project(m, lo + e)

    def groups(r):
        @pl.loop(0, N // 4)
        def _(i):
            for e in range(4):
                g = i * 4 + e
                grp[r][g] = tot[r][tab[LAST + g, 0]].astype(BF16).reshape(grp[r].shape[1:])

    def rr_copy(r, d, h, q, src):
        if q == 3:
            return rcopy(src.at[d], rr[r].at[d, h, q, d], rr_s.at[r, d], rr_r.at[r, d, spot(3 - h, q)], nbr[d])
        return rcopy(src, rr[r].at[d, h, q], rr_s.at[r, d], rr_r.at[r, d, spot(3 - h, q)], nbr[d])

    def ret_send(r, q):
        for d in (0, 1):
            rr_copy(r, d, 3 - q, q, grp[r].at[((5 + q) * sign[d]) % N]).start()

    def ret_own(r):
        for q in (3, 2, 1):
            ret_send(r, q)

    def ret_raw(r, part_no):
        for h, q in (((0, 3), (1, 2), (2, 1)), ((1, 3), (2, 2)), ((2, 3),))[part_no]:
            for d in (0, 1):
                rr_copy(r, d, h, q, rr[r].at[d, h, q]).wait_recv()
                rr_copy(r, d, h + 1, q, rr[r].at[d, h, q]).start()
        if part_no == 1:
            ret_send(r, 0)

    def rd_copy(r, d, u, s):
        return rcopy(sd[r].at[d, u, s], rd[r].at[d, u, s], rd_s.at[r, d], rd_r.at[r, d, u, s], nbr[d])

    def masked(flag, v):
        return jnp.where(flag, v, jnp.zeros_like(v))

    def ret_combine(r):
        for d in (0, 1):
            for q in (3, 2, 1, 0):
                rr_copy(r, d, 3, q, rr[r].at[d, 3, q]).wait_recv()
        for s in range(OWN):
            for d in (0, 1):
                o = at(4 * sign[d])
                acc = masked(sel(me, o) == s, grp[r][(4 * sign[d]) % N].astype(F32))
                for q in (0, 1, 2):
                    acc = acc + masked(sel(at(-(q + 1) * sign[d]), o) == s, rr[r][d, 3, q].astype(F32))
                far = masked(sel(at(-4 * sign[d]), o) == s, rr[r][d, 3, 3, d].astype(F32))
                sd[r][d, 0, s, d] = (acc[d] + far).astype(BF16)
                sd[r][d, 0, s, 1 - d] = acc[1 - d].astype(BF16)
                rd_copy(r, d, 0, s).start()

    def ret_dense(r, i):
        u, s = i // OWN, i % OWN
        for d in (0, 1):
            rd_copy(r, d, u, s).wait_recv()
            offset = (3 - u) * sign[d]
            own = grp[r][lax.rem(offset + N, N)].astype(F32)
            v = rd[r][d, u, s].astype(F32) + masked(sel(me, at(offset)) == s, own)
            sd[r][d, u + 1, s] = v.astype(BF16)
            rd_copy(r, d, u + 1, s).start()

    def ret_final(r):
        for s in range(OWN):
            v = masked(sel(me, me) == s, grp[r][0].astype(F32))
            for d in (0, 1):
                rd_copy(r, d, 3, s).wait_recv()
                v = v + rd[r][d, 3, s].astype(F32)
            out[r][s] = v.astype(BF16)

    def loop(lo, hi, f):
        if hi > lo:
            pl.loop(lo, hi)(f)

    copies[2].wait()
    for j in range(OWN):
        gather_first(0, j)
    copies[0].wait()
    copies[1].wait()
    move = build_tables()
    loop(0, 4, lambda i: gather_dense(0, i))
    for r in (0, 1):
        tot[r][2 * half] = jnp.zeros(tot[r].shape[1:], F32)
    move.wait()
    for cp in copies[3:]:
        cp.wait()
    loop(4, 12, lambda i: gather_dense(0, i))
    gather_select(0)
    gather_first(1, 0)
    gather_tail(0, lambda h: gather_first(1, h + 1))
    build(0)
    gather_dense(1, 0)
    project_part(0, theirs, 0)
    gather_dense(1, 1)
    project_part(0, theirs, 1)
    core1(0).start()
    gather_dense(1, 2)
    project_part(0, mine, 0)
    gather_dense(1, 3)
    project_part(0, mine, 1)
    gather_dense(1, 4)
    reduce_start(0)
    loop(5, 10, lambda i: gather_dense(1, i))
    reduce_mid(0)
    loop(10, 12, lambda i: gather_dense(1, i))
    gather_select(1)
    reduce_end(0)

    def fill(h):
        if h == 0:
            outer_part(0, mine, 0)
            outer_part(0, mine, 1)
            core2(0, theirs).wait_recv()
            outer_part(0, theirs, 0)
        elif h == 1:
            outer_part(0, theirs, 1)
            groups(0)
        else:
            ret_own(0)

    gather_tail(1, fill)
    build(1)
    project_part(1, theirs, 0)
    project_part(1, theirs, 1)
    core1(1).start()
    project_part(1, mine, 0)
    project_part(1, mine, 1)
    ret_raw(0, 0)
    ret_raw(0, 1)
    reduce_start(1)
    ret_raw(0, 2)
    ret_combine(0)
    loop(0, 4, lambda i: ret_dense(0, i))
    reduce_mid(1)
    loop(4, 9, lambda i: ret_dense(0, i))
    reduce_end(1)
    outer_part(1, mine, 0)
    outer_part(1, mine, 1)
    loop(9, 11, lambda i: ret_dense(0, i))
    core2(1, theirs).wait_recv()
    outer_part(1, theirs, 0)
    ret_dense(0, 11)
    outer_part(1, theirs, 1)
    groups(1)
    ret_own(1)
    for h in range(3):
        ret_raw(1, h)
    ret_combine(1)
    ret_final(0)
    loop(0, 12, lambda i: ret_dense(1, i))
    ret_final(1)

    for m in (0, 1):
        core1(m).wait_send()
        core2(m, mine).wait_send()
        if chips > 1:
            pieces_of(m, rs_s, rs_r).wait_send()
            pieces_of(m, ag_s, ag_r).wait_send()
        for d in (0, 1):
            for buf, sem in ((gd, gd_s), (rd, rd_s)):
                rcopy(buf[m].at[d], buf[m].at[d], sem.at[m, d], sem.at[m, d], nbr[d]).wait_send()
            for buf, sem in ((gs, gs_s), (rr, rr_s)):
                span = buf[m].at[d, pl.ds(0, 2)]
                rcopy(span, span, sem.at[m, d], sem.at[m, d], nbr[d]).wait_send()


def finish(a_ref, b_ref, oa_ref, ob_ref, a_buf, b_buf, sems):
    ways = ((a_ref, a_buf, oa_ref), (b_ref, b_buf, ob_ref))
    loads = [pltpu.make_async_copy(src, buf, sems.at[i]) for i, (src, buf, _) in enumerate(ways)]
    stores = [pltpu.make_async_copy(buf, dst, sems.at[2 + i]) for i, (_, buf, dst) in enumerate(ways)]
    for load in loads:
        load.start()
    for load, store in zip(loads, stores):
        load.wait()
        store.start()
    for store in stores:
        store.wait()


def body(chips, inputs, cotangent, factor_a, factor_b, adapter_slot, seg_adapter):
    segs = seg_adapter.shape[1]
    rows = inputs.shape[0] // segs
    feat = inputs.shape[1]
    per = -(-segs // (2 * chips))
    half = chips * per
    a_unit, b_unit = (2, feat // 2, 128), (2, 64, feat)
    bf = lambda *shape: pltpu.VMEM(shape, BF16)
    fl = lambda *shape: pltpu.VMEM(shape, F32)
    dma = lambda *shape: pltpu.SemaphoreType.DMA(shape)
    vm = pl.BlockSpec(memory_space=pltpu.VMEM)
    scratch = [
        bf(segs, rows, feat), bf(segs, rows, feat), bf(OWN, *a_unit), bf(OWN, *b_unit),
        pltpu.SMEM(adapter_slot.shape, jnp.int32), pltpu.VMEM(seg_adapter.shape, jnp.int32),
        bf(2, 4, 4, *a_unit), bf(2, 4, 4, *b_unit),
        bf(2, 4, 4, *a_unit), bf(2, 4, 4, *b_unit),
        bf(2, 4, *a_unit), bf(2, 4, *b_unit),
        bf(N, *a_unit), bf(N, *b_unit),
        fl(2, 2 * half, rows, 128), fl(2, half, rows, 128), bf(2, half, rows, 128),
        bf(2, chips, per, rows, 128), bf(2, 2 * half, rows, 128),
        fl(2 * half + 1, feat, 128), fl(2 * half + 1, 128, feat),
        bf(N, *a_unit), bf(N, *b_unit),
        bf(2, 4, 4, *a_unit), bf(2, 4, 4, *b_unit),
        bf(2, 4, 4, *a_unit), bf(2, 4, 4, *b_unit),
        bf(2, 4, 4, *a_unit), bf(2, 4, 4, *b_unit),
        pltpu.VMEM((64, 128), jnp.int32), pltpu.SMEM((64, 128), jnp.int32),
        dma(7),
        dma(2, 2), dma(2, 2, 4, 4), dma(2, 2), dma(2, 2, 10),
        dma(2, 2), dma(2, 2),
    ] + [dma(2)] * 8
    grad_a, grad_b = pl.pallas_call(
        functools.partial(kernel, segs, chips, per),
        out_shape=(
            jax.ShapeDtypeStruct((OWN,) + a_unit, BF16),
            jax.ShapeDtypeStruct((OWN,) + b_unit, BF16),
        ),
        in_specs=[
            pl.BlockSpec(memory_space=pl.ANY),
        ] * 6,
        out_specs=(vm, vm),
        scratch_shapes=scratch,
        compiler_params=pltpu.CompilerParams(
            collective_id=0, has_side_effects=True, vmem_limit_bytes=60 << 20
        ),
        name="adapter_backward",
    )(
        adapter_slot,
        seg_adapter,
        inputs.reshape(segs, rows, feat),
        cotangent.reshape(segs, rows, feat),
        factor_a.reshape((OWN,) + a_unit),
        factor_b.reshape((OWN,) + b_unit),
    )
    grad_a, grad_b = pl.pallas_call(
        finish,
        out_shape=(jax.ShapeDtypeStruct(grad_a.shape, BF16), jax.ShapeDtypeStruct(grad_b.shape, BF16)),
        in_specs=[pl.BlockSpec(memory_space=pl.ANY)] * 2,
        out_specs=(pl.BlockSpec(memory_space=pl.ANY),) * 2,
        scratch_shapes=[bf(OWN, *a_unit), bf(OWN, *b_unit), dma(4)],
        name="finish",
    )(grad_a, grad_b)
    return grad_a.reshape(factor_a.shape), grad_b.reshape(factor_b.shape)


def solution(mesh):
    return jax.shard_map(
        functools.partial(body, mesh.shape["tp"] // 2),
        mesh=mesh,
        in_specs=(
            P("grp", "tp"),
            P("grp", "tp"),
            P("grp", "tp", None),
            P("grp", None, "tp"),
            P(),
            P(),
        ),
        out_specs=(P("grp", "tp", None), P("grp", None, "tp")),
        check_vma=False,
    )
```
